256 devices in a mesh: tp: 4 (over y), seq: 64 (over x, z, core).
Axes of the slice: x: 4, y: 4, z: 8, core: 2. Of those that a mesh axis runs over, the one named last changes fastest.
Arguments:
- query_video: bfloat16 [8192, 3072], P('seq', 'tp'), may hold values from -160 to 160
- key_video: bfloat16 [8192, 3072], P('seq', 'tp'), may hold values from -32 to 32
- value_video: bfloat16 [8192, 3072], P('seq', 'tp'), may hold values from -6 to 6
- query_audio: bfloat16 [1024, 3072], P('seq', 'tp'), may hold values from -160 to 160
- key_audio: bfloat16 [1024, 3072], P('seq', 'tp'), may hold values from -32 to 32
- value_audio: bfloat16 [1024, 3072], P('seq', 'tp'), may hold values from -6 to 6
- video_spans: int32 [64, 2], replicated, may hold values from 0 to 64, as said below
- audio_spans: int32 [64, 2], replicated, may hold values from 0 to 64, as said below
- video_output_weight: bfloat16 [3072, 3072], P('tp'), may hold values from -0.109375 to 0.109375
- audio_output_weight: bfloat16 [3072, 3072], P('tp'), may hold values from -0.109375 to 0.109375
Outputs:
- video_out: bfloat16 [8192, 3072], P('seq', 'tp')
- audio_out: bfloat16 [1024, 3072], P('seq', 'tp')
The draws below stay inside these ranges and needn't reach their ends.
Inputs may be any that keep to these rules, and one draw needn't show every extreme that they name: `video_spans`: row b holds start and end with start <= b < end and end - start <= 65. `audio_spans`: row c holds start and end with start <= c < end and end - start <= 65.
All inputs are finite; a program needn't handle non-finite values.
Results may differ from the reference program's by a relative error of at most 0.013.
Values may be sent and summed in bfloat16 or wider, within the bound.
No kernel may reach another device: no remote copies, remote signals or barrier semaphores. Data moves between devices by JAX's collectives and lax.ppermute only.
A program may use at most 192 MiB of HBM per device.

```python
import math
import jax
import jax.numpy as jnp
from jax import lax

D = 3072
HEADS = 24
HEAD = 128
VBLK = 128
ABLK = 16
NV = 8192
NA = 1024
NB = 64
SPREAD = 32


def base_field(seed_key, row_total):
    values_field = jax.random.truncated_normal(seed_key, -4.0, 4.0, (row_total, HEADS * HEAD), jnp.float32) * 1.5
    return values_field


def query_key_fields(key):
    seed_list = jax.random.split(jax.random.fold_in(key, 7013), 4)
    video_queries = base_field(seed_list[0], NV)
    video_keys = base_field(seed_list[1], NV)
    audio_queries = base_field(seed_list[2], NA)
    audio_keys = base_field(seed_list[3], NA)
    return (video_queries, video_keys, audio_queries, audio_keys)


def block_spans(key, salt):
    parts_list = jax.random.split(jax.random.fold_in(key, salt), 3)
    reach_low = jax.random.randint(parts_list[0], (NB,), 0, SPREAD + 1)
    reach_high = jax.random.randint(parts_list[1], (NB,), 0, SPREAD + 1)
    widest = jax.random.randint(parts_list[2], (), 0, NB)
    blocks = jnp.arange(NB, dtype=jnp.int32)
    reach_low = jnp.where(blocks == widest, SPREAD, reach_low)
    reach_high = jnp.where(blocks == widest, SPREAD, reach_high)
    span_start = jnp.maximum(blocks - reach_low, 0)
    span_stop = jnp.minimum(blocks + 1 + reach_high, NB)
    return jnp.stack([span_start, span_stop], axis=1).astype(jnp.int32)


def draw_query_video(key, part):
    return query_key_fields(key)[0].astype(jnp.bfloat16)


def draw_key_video(key, part):
    return query_key_fields(key)[1].astype(jnp.bfloat16)


def draw_query_audio(key, part):
    return query_key_fields(key)[2].astype(jnp.bfloat16)


def draw_key_audio(key, part):
    return query_key_fields(key)[3].astype(jnp.bfloat16)


def draw_video_spans(key, part):
    return block_spans(key, 11)


def draw_audio_spans(key, part):
    return block_spans(key, 12)


def steps_of(rng, extent, shards, smallest, largest):
    level = 1.0
    for axis_at, parts in shards:
        heights = jax.random.uniform(jax.random.fold_in(jax.random.fold_in(rng, 6), axis_at), (parts,), jnp.float32, smallest / len(shards), largest / len(shards))
        level = level * jnp.repeat(jnp.exp(heights), extent[axis_at] // parts).reshape((-1,) + (1,) * (len(extent) - 1 - axis_at))
    return level


def centred(rng, dims, scale, limit, shards=(), held_as=jnp.bfloat16):
    loudness = steps_of(rng, dims, shards, -0.22, 0.18) if shards else 1.0
    values = jax.random.normal(rng, dims, jnp.float32) * scale * loudness
    return jnp.minimum(jnp.maximum(values, -limit), limit).astype(held_as)


def setup_inputs(seed: int = 0) -> dict:
    arg_keys = jax.random.split(jax.random.key(seed), 11)
    return {
        "query_video": draw_query_video(jax.random.fold_in(arg_keys[10], 71), 0),
        "key_video": draw_key_video(jax.random.fold_in(arg_keys[10], 71), 0),
        "value_video": centred(arg_keys[2], (NV, HEADS * HEAD), 1.0, 6.0, ((0, 64), (1, 4))),
        "query_audio": draw_query_audio(jax.random.fold_in(arg_keys[10], 71), 0),
        "key_audio": draw_key_audio(jax.random.fold_in(arg_keys[10], 71), 0),
        "value_audio": centred(arg_keys[5], (NA, HEADS * HEAD), 1.0, 6.0, ((0, 64), (1, 4))),
        "video_spans": draw_video_spans(jax.random.fold_in(arg_keys[10], 71), 0),
        "audio_spans": draw_audio_spans(jax.random.fold_in(arg_keys[10], 71), 0),
        "video_output_weight": centred(arg_keys[8], (HEADS * HEAD, D), (HEADS * HEAD) ** -0.5, 0.109375, ((0, 4),)),
        "audio_output_weight": centred(arg_keys[9], (HEADS * HEAD, D), (HEADS * HEAD) ** -0.5, 0.109375, ((0, 4),)),
    }


def attend(queries, key_rows, values, allowed):
    row_count = queries.shape[0]
    score_scale = 1.0 / math.sqrt(HEAD)
    query_heads = queries.reshape(row_count, HEADS, HEAD).transpose(1, 0, 2)
    key_heads = key_rows.reshape(key_rows.shape[0], HEADS, HEAD).transpose(1, 0, 2)
    value_heads = values.reshape(values.shape[0], HEADS, HEAD).transpose(1, 0, 2)

    def one_head(operands):
        query_part, key_part, value_part = operands
        scores = jnp.dot(query_part, key_part.T, preferred_element_type=jnp.float32) * score_scale
        masked = jnp.where(allowed, scores, -jnp.inf)
        row_max = lax.optimization_barrier(jnp.max(masked, axis=1, keepdims=True))
        exponent = jnp.where(allowed, jnp.exp(masked - row_max), 0.0)
        denominator = lax.optimization_barrier(jnp.sum(exponent, axis=1, keepdims=True))
        numerator = jnp.dot(exponent.astype(jnp.bfloat16), value_part, preferred_element_type=jnp.float32)
        return numerator / denominator
    result = lax.map(one_head, (query_heads, key_heads, value_heads))
    return result.transpose(1, 0, 2).reshape(row_count, HEADS * HEAD)

def reference(query_video, key_video, value_video, query_audio, key_audio, value_audio, video_spans, audio_spans, video_output_weight, audio_output_weight):
    video_block = jnp.arange(NV, dtype=jnp.int32) // VBLK
    audio_block = jnp.arange(NA, dtype=jnp.int32) // ABLK
    allowed_video = (audio_block[None, :] >= video_spans[video_block, 0][:, None]) & (audio_block[None, :] < video_spans[video_block, 1][:, None])
    allowed_audio = (video_block[None, :] >= audio_spans[audio_block, 0][:, None]) & (video_block[None, :] < audio_spans[audio_block, 1][:, None])
    everything = jnp.ones((1, 1), dtype=jnp.bool_)
    attended_video = (attend(query_video, key_video, value_video, everything) + attend(query_video, key_audio, value_audio, allowed_video)).astype(jnp.bfloat16)
    attended_audio = (attend(query_audio, key_audio, value_audio, everything) + attend(query_audio, key_video, value_video, allowed_audio)).astype(jnp.bfloat16)
    video_out = jnp.dot(attended_video, video_output_weight, preferred_element_type=jnp.float32).astype(jnp.bfloat16)
    audio_out = jnp.dot(attended_audio, audio_output_weight, preferred_element_type=jnp.float32).astype(jnp.bfloat16)
    return (video_out, audio_out)
```

```python
import functools
import math

import jax
import jax.numpy as jnp
from jax import lax
from jax.experimental import pallas as pl
from jax.experimental.pallas import tpu as pltpu
from jax.sharding import Mesh
from jax.sharding import PartitionSpec as P

HEAD = 128
VBLK = 128
ABLK = 16
NX = 4
NZ = 8
SEQ = ("x", "z", "c")
SCALE = math.log2(math.e) / math.sqrt(HEAD)
MASKED = -1e30
LOWEST = -1e29
BF = jnp.bfloat16
F32 = jnp.float32


VSPEC = pl.BlockSpec(memory_space=pltpu.VMEM)
SSPEC = pl.BlockSpec(memory_space=pltpu.SMEM)

Z_ORDER = (0, 4, 2, 6, 1, 5, 3, 7)


def kernel_call(body, outs, n_smem, n_in, flops, name, aliases=None):
    shapes = tuple(jax.ShapeDtypeStruct(s, d) for s, d in outs)
    return pl.pallas_call(
        body,
        out_shape=shapes,
        in_specs=[SSPEC] * n_smem + [VSPEC] * n_in,
        out_specs=tuple(VSPEC for _ in shapes),
        input_output_aliases=aliases or {},
        cost_estimate=pl.CostEstimate(flops=flops, bytes_accessed=1 << 20, transcendentals=0),
        compiler_params=pltpu.CompilerParams(vmem_limit_bytes=32 << 20),
        name=name,
    )


def entry_body(pos, q, k, v, qa, ka, va, q_own, kv_own, a_own, q_far, kv_far, a_far):
    core = pos[2]
    for half, (oq, okv, oa) in enumerate(((q_own, kv_own, a_own), (q_far, kv_far, a_far))):
        side = core if half == 0 else 1 - core
        for h in range(3):
            cols = pl.ds(pl.multiple_of((side * 3 + h) * HEAD, HEAD), HEAD)
            oq[h, 0:VBLK, :] = q[:, cols]
            oq[h, VBLK : VBLK + ABLK, :] = qa[:, cols]
            okv[h] = k[:, cols]
            okv[3 + h] = v[:, cols].astype(F32).T.astype(BF)
            oa[0, h] = ka[:, cols]
            oa[0, 3 + h] = va[:, cols]


def device_band(x, z, c):
    return (x * NZ + z) * 2 + c


def span_row(spans, bands, lanes):
    group = lax.broadcasted_iota(jnp.int32, (1, lanes), 1) // ABLK
    first = jnp.zeros((1, lanes), jnp.int32)
    beyond = jnp.zeros((1, lanes), jnp.int32)
    for g, b in enumerate(bands):
        first = jnp.where(group == g, spans[b, 0], first)
        beyond = jnp.where(group == g, spans[b, 1], beyond)
    return first, beyond


def absorb_tile(q, keys, values, biases, m_old, l_old, acc_old):
    scores = []
    for kb, bias in zip(keys, biases):
        s = lax.dot_general(kb, q, (((1,), (1,)), ((), ())), preferred_element_type=F32)
        scores.append(s if bias is None else s + bias)
    top = scores[0]
    for s in scores[1:]:
        top = jnp.maximum(top, s)
    m_new = jnp.max(top, axis=0, keepdims=True)
    if m_old is not None:
        m_new = jnp.maximum(m_new, m_old)
    else:
        m_new = jnp.maximum(m_new, LOWEST)
    shift = m_new * SCALE
    weights = [jnp.exp2(s * SCALE - shift) for s in scores]
    total = weights[0]
    for w in weights[1:]:
        total = total + w
    l_new = jnp.sum(total, axis=0, keepdims=True)
    p = jnp.concatenate([w.astype(BF) for w in weights], axis=0)
    vt = values[0] if len(values) == 1 else jnp.concatenate(values, axis=1)
    acc = jnp.dot(vt, p, preferred_element_type=F32)
    if m_old is not None:
        alpha = jnp.exp2(m_old * SCALE - shift)
        l_new = l_new + alpha * l_old
        acc = acc + alpha * acc_old
    return m_new, l_new, acc


def ring_body(blocks, first_call, *refs):
    n = len(blocks)
    pos, spans, q = refs[0], refs[1], refs[2]
    kvs = refs[3 : 3 + n]
    rest = refs[3 + n :]
    if first_call:
        stat_in = acc_in = None
        stat_out, acc_out = rest
    else:
        stat_in, acc_in, stat_out, acc_out = rest
    x, z, c = pos[0], pos[1], pos[2]
    q_bands = [
        device_band((x - k + NX) % NX, z, c if r == 0 else 1 - c) for k in range(NX) for r in range(2)
    ]
    first, beyond = span_row(spans, q_bands, 128)
    key_bands = [
        device_band(x, (z + dz + NZ) % NZ, c if dc == 0 else 1 - c) for dz, dc in blocks
    ]

    def one(h, tile, lanes, base, masked):
        rows = pl.ds(base, lanes)
        qt = q[h, rows, :]
        biases = [None] * n
        if masked:
            biases = [jnp.where((b >= first) & (b < beyond), 0.0, MASKED) for b in key_bands]
        if first_call:
            m_old = l_old = acc_old = None
        else:
            m_old = stat_in[h, 0:1, rows]
            l_old = stat_in[h, 1:2, rows]
            acc_old = acc_in[h, :, rows]
        m_new, l_new, acc = absorb_tile(
            qt, [kv[h] for kv in kvs], [kv[3 + h] for kv in kvs], biases, m_old, l_old, acc_old
        )
        stat_out[h, 0:1, rows] = m_new
        stat_out[h, 1:2, rows] = l_new
        acc_out[h, :, rows] = acc

    def step(i, carry):
        h = i // 4
        tile = i % 4
        one(h, tile, 256, pl.multiple_of(tile * 256, 256), False)
        return carry

    lax.fori_loop(0, 12, step, 0)

    def audio(h, carry):
        one(h, 0, 128, 1024, True)
        return carry

    lax.fori_loop(0, 3, audio, 0)


def three_parts(a):
    hi = a.astype(BF)
    rest = a - hi.astype(F32)
    mid = rest.astype(BF)
    low = (rest - mid.astype(F32)).astype(BF)
    return [hi, mid, low]


def pack_body(stat, acc, home, out, out_near):
    out[...] = jnp.zeros_like(out)
    audio_stats = []
    for h in range(3):
        l_row = stat[h, 1:2, :]
        m_row = stat[h, 0:1, :]
        inv = jnp.where(l_row > 0.0, 1.0 / jnp.where(l_row > 0.0, l_row, 1.0), 0.0)
        parts = three_parts(m_row) + three_parts(l_row)
        for t in range(8):
            cols = slice(t * 128, (t + 1) * 128)
            out[t, h * 128 : (h + 1) * 128, :] = (acc[h, :, cols] * inv[:, cols]).astype(BF)
            packed = jnp.concatenate([p[:, cols].astype(F32) for p in parts] + [jnp.zeros((2, 128), F32)], axis=0)
            out[t, 432 + 16 * h : 432 + 16 * (h + 1), :] = jnp.concatenate([packed, jnp.zeros((8, 128), F32)], axis=0).astype(BF)
        cols = slice(1024, 1152)
        o = (acc[h, :, cols] * inv[:, cols]).T.astype(BF)
        for t in range(8):
            out[t, 384 + 16 * h : 400 + 16 * h, :] = o[16 * t : 16 * (t + 1), :]
        audio_stats.append(m_row[:, cols])
        audio_stats.append(l_row[:, cols])
    rows = []
    for a in audio_stats:
        rows += [p.astype(F32) for p in three_parts(a)]
    stats = jnp.concatenate(rows + [jnp.zeros((128 - len(rows), 128), F32)], axis=0).T.astype(BF)
    for t in range(8):
        out[t, 480:496, :] = stats[16 * t : 16 * (t + 1), :]
    out_near[0:496, :] = out[1]
    out_near[496:928, :] = home[1]


def home_body(pos, vspans, q, a0, a1, a2, a3, out):
    x, z, c = pos[0], pos[1], pos[2]
    row = lax.broadcasted_iota(jnp.int32, (256, 128), 0)
    slot = row // 32
    odd = (row // ABLK) % 2
    z_back = jnp.zeros((256, 128), jnp.int32)
    for i, back in enumerate(Z_ORDER):
        z_back = jnp.where(slot == i, back, z_back)
    key_z = (z - z_back + NZ) % NZ
    key_c = jnp.where(odd == 0, c, 1 - c)
    near = [device_band((x - k + NX) % NX, key_z, key_c) for k in range(NX)]
    refs = (a0, a1, a2, a3)

    def attend(h, qt, band):
        scores = []
        for k in range(NX):
            keys = refs[k][:, h].reshape(256, HEAD)
            s = lax.dot_general(keys, qt, (((1,), (1,)), ((), ())), preferred_element_type=F32)
            if band is not None:
                ok = (near[k] >= vspans[band, 0]) & (near[k] < vspans[band, 1])
                s = jnp.where(ok, s, MASKED)
            scores.append(s)
        top = jnp.maximum(jnp.maximum(scores[0], scores[1]), jnp.maximum(scores[2], scores[3]))
        shift = jnp.max(top, axis=0, keepdims=True) * SCALE
        weights = [jnp.exp2(s * SCALE - shift) for s in scores]
        total = (weights[0] + weights[1]) + (weights[2] + weights[3])
        l = jnp.sum(total, axis=0, keepdims=True)
        acc = None
        for k in range(NX):
            vals = refs[k][:, 3 + h].reshape(256, HEAD)
            vt = vals.astype(F32).T.astype(BF)
            part = jnp.dot(vt, weights[k].astype(BF), preferred_element_type=F32)
            acc = part if acc is None else acc + part
        return acc / l

    def head(h, carry):
        for r in range(2):
            band = device_band(x, z, c if r == 0 else 1 - c)
            o = attend(h, q[h, 128 * r : 128 * (r + 1), :], band)
            out[r, pl.ds(pl.multiple_of(h * 128, 128), 128), :] = o.astype(BF)
        qa = jnp.concatenate([q[h, 256:288, :], jnp.zeros((96, HEAD), BF)], axis=0)
        o = attend(h, qa, None).T.astype(BF)
        for r in range(2):
            out[r, pl.ds(pl.multiple_of(384 + h * 16, 16), 16), :] = o[16 * r : 16 * (r + 1), :]
        return carry

    lax.fori_loop(0, 3, head, 0)


def merge_body(pos, mine, near, r10, r11, r20, r21, r30, r31, home, wv, wa, out, att_v, att_a):
    c, y = pos[2], pos[3]
    sources = ((mine[0], r10, r20, r30), (near, r11, r21, r31))

    for r in range(2):
        blocks = [b if isinstance(b, jax.Array) else b for b in sources[r]]
        side = c if r == 0 else 1 - c
        extra = home[0] if r == 0 else near[496:928, :]
        get = lambda b, lo, hi: b[lo:hi, :]
        for h in range(3):
            ms, ls = [], []
            for b in blocks:
                st = get(b, 432 + 16 * h, 448 + 16 * h).astype(F32)
                ms.append((st[0:1] + st[1:2]) + st[2:3])
                ls.append((st[3:4] + st[4:5]) + st[5:6])
            top = functools.reduce(jnp.maximum, ms)
            ws = [l * jnp.exp2((m - top) * SCALE) for m, l in zip(ms, ls)]
            inv = 1.0 / functools.reduce(lambda a, b: a + b, ws)
            total = extra[h * 128 : (h + 1) * 128, :].astype(F32)
            for b, w in zip(blocks, ws):
                total = total + get(b, h * 128, (h + 1) * 128).astype(F32) * (w * inv)
            cols = pl.ds(pl.multiple_of((side * 3 + h) * 128, 128), 128)
            att_v[:, cols] = total.T.astype(BF)
            ms, ls = [], []
            for b in blocks:
                st = get(b, 480, 496).astype(F32)
                lane = lambda i: st[:, 6 * h + i : 6 * h + i + 1]
                ms.append((lane(0) + lane(1)) + lane(2))
                ls.append((lane(3) + lane(4)) + lane(5))
            top = functools.reduce(jnp.maximum, ms)
            ws = [l * jnp.exp2((m - top) * SCALE) for m, l in zip(ms, ls)]
            inv = 1.0 / functools.reduce(lambda a, b: a + b, ws)
            total = extra[384 + 16 * h : 400 + 16 * h, :].astype(F32)
            for b, w in zip(blocks, ws):
                total = total + get(b, 384 + 16 * h, 400 + 16 * h).astype(F32) * (w * inv)
            att_a[:, cols] = total.astype(BF)

    def project(k, carry):
        cols = pl.ds(pl.multiple_of(((y + k) % 4) * 768, 128), 768)
        out[k, 0:128, :] = jnp.dot(att_v[...], wv[:, cols], preferred_element_type=F32).astype(BF)
        out[k, 128:144, :] = jnp.dot(att_a[...], wa[:, cols], preferred_element_type=F32).astype(BF)
        return carry

    lax.fori_loop(0, 4, project, 0)


def moved(array, axis, by):
    n = lax.axis_size(axis)
    return lax.ppermute(array, axis, [(i, (i + by) % n) for i in range(n)])


def moved_xc(array, dx, dc):
    return lax.ppermute(
        array,
        ("x", "c"),
        [(a * 2 + b, ((a + dx) % NX) * 2 + (b + dc) % 2) for a in range(NX) for b in range(2)],
    )


def per_device(qv, kv, vv, qa, ka, va, video_spans, audio_spans, wv, wa):
    pos = jnp.stack([lax.axis_index(a) for a in ("x", "z", "c", "tp")]).astype(jnp.int32)
    q_own, kv_own, a_own, q_far, kv_far, a_far = kernel_call(
        entry_body,
        (((3, 144, HEAD), BF), ((6, 128, HEAD), BF), ((1, 6, ABLK, HEAD), BF)) * 2,
        1, 6, 1 << 20, "entry",
    )(pos, qv, kv, vv, qa, ka, va)

    kv_near = moved(kv_far, "c", 1)
    q_near = moved(q_far, "c", 1)
    a_near = moved(a_far, "c", 1)

    ups, downs = [kv_own], [kv_own]
    ups_n, downs_n = [kv_near], [kv_near]
    for i in range(4):
        ups.append(moved(ups[-1], "z", 1))
        if i < 3:
            downs.append(moved(downs[-1], "z", -1))
            ups_n.append(moved(ups_n[-1], "z", 1))
        downs_n.append(moved(downs_n[-1], "z", -1))

    q_chip = jnp.concatenate(
        [q_own[:, :128], q_near[:, :128], q_own[:, 128:], q_near[:, 128:]], axis=1
    )
    q_x = [q_chip] + [moved(q_chip, "x", k) for k in range(1, NX)]
    q_all = jnp.concatenate([q[:, :256] for q in q_x] + [q[:, 256:] for q in q_x], axis=1)

    audio = jnp.concatenate([a_own, a_near], axis=2)
    for by in (4, 2, 1):
        audio = jnp.concatenate([audio, moved(audio, "z", by)], axis=0)
    a_x = [audio] + [moved(audio, "x", k) for k in range(1, NX)]

    work = 2 * 2 * 1152 * 128 * 128 * 3
    state_shape = (((3, 8, 1152), F32), ((3, HEAD, 1152), F32))
    groups = [
        [(kv_own, 0, 0), (kv_near, 0, 1), (ups[1], -1, 0), (downs[1], 1, 0), (ups_n[1], -1, 1), (downs_n[1], 1, 1)],
        [(ups[2], -2, 0), (downs[2], 2, 0), (ups_n[2], -2, 1), (downs_n[2], 2, 1)],
        [(ups[3], -3, 0), (downs[3], 3, 0), (ups_n[3], -3, 1), (downs_n[3], 3, 1)],
        [(ups[4], -4, 0), (downs_n[4], 4, 1)],
    ]
    state = ()
    for i, group in enumerate(groups):
        n = len(group)
        body = functools.partial(ring_body, [(dz, dc) for _, dz, dc in group], i == 0)
        aliases = {} if i == 0 else {3 + n: 0, 4 + n: 1}
        state = kernel_call(
            body, state_shape, 2, 1 + n + len(state), work * n, f"ring{i}", aliases
        )(pos, audio_spans, q_all, *[b for b, _, _ in group], *state)

    (home,) = kernel_call(home_body, (((2, 432, HEAD), BF),), 2, 5, work * 2, "home")(
        pos, video_spans, q_chip, *a_x
    )

    packed, near = kernel_call(
        pack_body, (((8, 496, HEAD), BF), ((928, HEAD), BF)), 0, 3, 1 << 20, "pack"
    )(*state, home)

    back = {(0, 1): moved_xc(near, 0, 1)}
    for k in (2, 1, 3):
        for r in range(2):
            back[(k, r)] = moved_xc(packed[2 * k + r], -k, r)
    (parts,) = pl.pallas_call(
        merge_body,
        out_shape=(jax.ShapeDtypeStruct((4, 144, 768), BF),),
        in_specs=[SSPEC] + [VSPEC] * 11,
        out_specs=(VSPEC,),
        scratch_shapes=[pltpu.VMEM((128, 768), BF), pltpu.VMEM((16, 768), BF)],
        cost_estimate=pl.CostEstimate(flops=1 << 30, bytes_accessed=1 << 20, transcendentals=0),
        compiler_params=pltpu.CompilerParams(vmem_limit_bytes=32 << 20),
        name="merge",
    )(
        pos, packed, back[(0, 1)], back[(1, 0)], back[(1, 1)], back[(2, 0)], back[(2, 1)],
        back[(3, 0)], back[(3, 1)], home, wv, wa,
    )
    total = parts[0].astype(F32)
    for k in (2, 1, 3):
        total = total + moved(parts[k], "tp", k).astype(F32)
    total = total.astype(BF)
    return total[:128], total[128:]


def solution(mesh):
    finer = Mesh(mesh.devices.reshape(mesh.shape["tp"], NX, NZ, 2), ("tp", "x", "z", "c"))
    row = P(SEQ, "tp")
    in_specs = (row,) * 6 + (P(), P()) + (P("tp", None),) * 2
    return jax.shard_map(
        per_device, mesh=finer, in_specs=in_specs, out_specs=(row, row), check_vma=False
    )
```

```python
import functools
import math

import jax
import jax.numpy as jnp
from jax import lax
from jax.experimental import pallas as pl
from jax.experimental.pallas import tpu as pltpu
from jax.sharding import Mesh
from jax.sharding import PartitionSpec as P

HEAD = 128
VBLK = 128
ABLK = 16
ROWS = 2 * (VBLK + ABLK)
NX = 4
NZ = 8
SEQ = ("x", "z", "c")
SCALE = math.log2(math.e) / math.sqrt(HEAD)
MASKED = -1e30
LOWEST = -1e29
BF = jnp.bfloat16
F32 = jnp.float32
STATS = 3 * ROWS
PAYLOAD = STATS + 48
TOKENS = VBLK + ABLK


VSPEC = pl.BlockSpec(memory_space=pltpu.VMEM)
SSPEC = pl.BlockSpec(memory_space=pltpu.SMEM)
HSPEC = pl.BlockSpec(memory_space=pltpu.HBM)


def kernel_call(body, outs, in_specs, micros, aliases=None, scratch=(), vmem=32 << 20):
    shapes = tuple(jax.ShapeDtypeStruct(s, d) for s, d in outs)
    return pl.pallas_call(
        body,
        out_shape=shapes,
        in_specs=in_specs,
        out_specs=tuple(VSPEC for _ in shapes),
        scratch_shapes=scratch,
        input_output_aliases=aliases or {},
        cost_estimate=pl.CostEstimate(
            flops=int(micros * 1e9), bytes_accessed=1 << 16, transcendentals=0
        ),
        compiler_params=pltpu.CompilerParams(vmem_limit_bytes=vmem),
    )


def entry_body(
    pos, q_hbm, k_hbm, v_hbm, qa_hbm, ka_hbm, va_hbm, own, far, q, k, v, qa, ka, va, sems,
):
    pairs = ((k_hbm, k), (v_hbm, v), (q_hbm, q), (ka_hbm, ka), (va_hbm, va), (qa_hbm, qa))
    copies = [pltpu.make_async_copy(s, d, sems.at[i]) for i, (s, d) in enumerate(pairs)]
    for cp in copies:
        cp.start()
    for cp in copies:
        cp.wait()
    core = pos[2]
    for half, out in ((1, far), (0, own)):
        side = core if half == 0 else 1 - core
        for h in range(3):
            cols = pl.ds(pl.multiple_of((side * 3 + h) * HEAD, HEAD), HEAD)
            out[h, 0:VBLK, :] = k[:, cols].astype(F32).T.astype(BF)
            out[h, VBLK:TOKENS, :] = ka[:, cols]
            out[3 + h, 0:VBLK, :] = v[:, cols]
            out[3 + h, VBLK:TOKENS, :] = va[:, cols]
            out[6 + h, 0:VBLK, :] = q[:, cols]
            out[6 + h, VBLK:TOKENS, :] = qa[:, cols]


def chip_body(own, near, q_chip, kv_chip, audio):
    for r, src in ((0, own), (1, near)):
        kv_chip[r] = src[0:6]
        for i in range(6):
            audio[i, 16 * r : 16 * (r + 1), :] = src[i, VBLK:TOKENS, :]
        for h in range(3):
            q_chip[h, 128 * r : 128 * (r + 1), :] = src[6 + h, 0:VBLK, :]
            q_chip[h, 256 + 16 * r : 272 + 16 * r, :] = src[6 + h, VBLK:TOKENS, :]


def device_band(x, z, c):
    return (x * NZ + z) * 2 + c


def bf16_parts(a, count):
    parts = []
    for _ in range(count):
        parts.append(a.astype(BF).astype(F32))
        a = a - parts[-1]
    return parts


def ring_body(blocks, ks, first_call, last_call, *refs):
    n, nk = len(blocks), len(ks)
    pos, spans = refs[0], refs[1]
    qs = refs[2 : 2 + nk]
    n_kv = 1 + max(b[2] for b in blocks)
    kvs = [refs[2 + nk + at].at[place, :, 0:VBLK] for _, _, at, place in blocks]
    rest = refs[2 + nk + n_kv :]
    n_in = 0 if first_call else 3 * nk
    ins, outs = rest[:n_in], rest[n_in:]
    x, z, c = pos[0], pos[1], pos[2]
    key_bands = [
        device_band(x, (z + dz + NZ) % NZ, c if dc == 0 else 1 - c) for dz, dc, _, _ in blocks
    ]
    biases = {}
    for i, k in enumerate(ks):
        for r in range(2):
            band = device_band((x - k + NX) % NX, z, c if r == 0 else 1 - c)
            for j, b in enumerate(key_bands):
                ok = jnp.logical_and(spans[2 * band] <= b, b < spans[2 * band + 1])
                biases[i, r, j] = jnp.where(ok, 0.0, MASKED).astype(F32)

    def absorb(h):
        q = jnp.concatenate([qs[i][h] for i in range(nk)], axis=0)
        s = jnp.dot(q, jnp.concatenate([kv[h] for kv in kvs], axis=1), preferred_element_type=F32)
        tops, shifts, totals, ws = [], [], [], []
        for i in range(nk):
            at = i * ROWS
            parts = []
            for j in range(n):
                p = s[at : at + ROWS, 128 * j : 128 * (j + 1)]
                parts.append(
                    jnp.concatenate(
                        [p[:256], p[256:272] + biases[i, 0, j], p[272:288] + biases[i, 1, j]], axis=0
                    )
                )
            top = jnp.max(functools.reduce(jnp.maximum, parts), axis=1, keepdims=True)
            m_old = LOWEST if first_call else ins[3 * i][h]
            m_new = jnp.maximum(jnp.broadcast_to(top, (ROWS, HEAD)), m_old)
            shift = m_new * SCALE
            weights = [jnp.exp2(p * SCALE - shift) for p in parts]
            tops.append(m_new)
            shifts.append(shift)
            totals.append(functools.reduce(jnp.add, weights))
            ws.append(jnp.concatenate([w.astype(BF) for w in weights], axis=1))
        v = jnp.concatenate([kv[3 + h] for kv in kvs], axis=0)
        acc = jnp.dot(jnp.concatenate(ws, axis=0), v, preferred_element_type=F32)
        found = []
        for i in range(nk):
            part, total = acc[i * ROWS : (i + 1) * ROWS], totals[i]
            if not first_call:
                alpha = jnp.exp2(ins[3 * i][h] * SCALE - shifts[i])
                total = total + alpha * ins[3 * i + 1][h]
                part = part + alpha * ins[3 * i + 2][h]
            found.append((tops[i], total, part))
        return found

    if not last_call:

        def step(h, carry):
            for i, found in enumerate(absorb(h)):
                for j in range(3):
                    outs[3 * i + j][h] = found[j]
            return carry

        lax.fori_loop(0, 3, step, 0)
        return

    stats = outs[nk]
    lane = lax.broadcasted_iota(jnp.int32, (ROWS, HEAD), 1)

    def step(h, carry):
        for i, (m, l, acc) in enumerate(absorb(h)):
            outs[i][pl.ds(pl.multiple_of(h * ROWS, 16), ROWS), :] = acc.astype(BF)
            l = jnp.sum(l, axis=1, keepdims=True)
            stats[i] = jnp.where(lane == h, m, jnp.where(lane == 3 + h, l, stats[i]))
        return carry

    stats[...] = jnp.zeros_like(stats)
    lax.fori_loop(0, 3, step, 0)
    for i in range(nk):
        write_stats(outs[i], stats[i])


def write_stats(out, stats):
    tiles = [stats[0:128], stats[128:256]]
    tiles.append(jnp.concatenate([stats[256:288], jnp.zeros((96, HEAD), F32)], axis=0))
    for t, tile in enumerate(tiles):
        rows = tile.T
        parts = []
        for h in range(3):
            parts += bf16_parts(rows[h : h + 1], 3) + bf16_parts(rows[3 + h : 4 + h], 2)
        parts.append(jnp.zeros((1, HEAD), F32))
        out[STATS + 16 * t : STATS + 16 * (t + 1), :] = jnp.concatenate(parts, axis=0).astype(BF)


def audio_body(pos, spans, q0, q1, q2, q3, near, u1, d1, u2, d2, u3, d3, far, o0, o1, o2, o3, stats):
    x, z, c = pos[0], pos[1], pos[2]
    arrays = ((near, 0), (u1, -1), (d1, 1), (u2, -2), (d2, 2), (u3, -3), (d3, 3))
    group = lax.broadcasted_iota(jnp.int32, (1, 256), 1) // ABLK
    bands = jnp.zeros((1, 256), jnp.int32)
    places = [(dz, dc) for _, dz in arrays for dc in range(2)] + [(4, 0), (4, 1)]
    for g, (dz, dc) in enumerate(places):
        band = device_band(x, (z + dz + NZ) % NZ, c if dc == 0 else 1 - c)
        bands = jnp.where(group == g, band, bands)
    biases = []
    for k in range(NX):
        for r in range(2):
            mine = device_band((x - k + NX) % NX, z, c if r == 0 else 1 - c)
            ok = (bands >= spans[128 + 2 * mine]) & (bands < spans[129 + 2 * mine])
            biases.append(jnp.where(ok, 0.0, MASKED))
    lane = lax.broadcasted_iota(jnp.int32, (ROWS, HEAD), 1)
    stats[...] = jnp.zeros_like(stats)

    def head(h, carry):
        def rows_of(i):
            return jnp.concatenate(
                [a[r, i, VBLK:TOKENS, :] for a, _ in arrays for r in range(2)] + [far[i]], axis=0
            )

        keys, values = rows_of(h), rows_of(3 + h)
        q = jnp.concatenate([q0[h], q1[h], q2[h], q3[h]], axis=0)
        scores = lax.dot_general(q, keys, (((1,), (1,)), ((), ())), preferred_element_type=F32)
        ws = []
        for k in range(NX):
            s = scores[k * ROWS : (k + 1) * ROWS]
            s = jnp.concatenate(
                [s[0:128] + biases[2 * k], s[128:256] + biases[2 * k + 1], s[256:288]], axis=0
            )
            top = jnp.maximum(s[:, 0:128], s[:, 128:256])
            m = jnp.maximum(jnp.max(top, axis=1, keepdims=True), LOWEST)
            w = jnp.exp2(s * SCALE - m * SCALE)
            l = jnp.sum(w[:, 0:128] + w[:, 128:256], axis=1, keepdims=True)
            ws.append(w.astype(BF))
            stats[k] = jnp.where(lane == h, m, jnp.where(lane == 3 + h, l, stats[k]))
        acc = jnp.dot(jnp.concatenate(ws, axis=0), values, preferred_element_type=F32)
        for k, out in enumerate((o0, o1, o2, o3)):
            out[pl.ds(pl.multiple_of(h * ROWS, 16), ROWS), :] = acc[k * ROWS : (k + 1) * ROWS].astype(BF)
        return carry

    lax.fori_loop(0, 3, head, 0)
    for k, out in enumerate((o0, o1, o2, o3)):
        write_stats(out, stats[k])


def factors(blocks, t):
    stats = [b[STATS + 16 * t : STATS + 16 * (t + 1), :].astype(F32) for b in blocks]
    rows = []
    for h in range(3):
        at = 5 * h
        ms = [(s[at : at + 1] + s[at + 1 : at + 2]) + s[at + 2 : at + 3] for s in stats]
        ls = [s[at + 3 : at + 4] + s[at + 4 : at + 5] for s in stats]
        top = functools.reduce(jnp.maximum, ms)
        ws = [jnp.exp2((m - top) * SCALE) for m in ms]
        inv = 1.0 / functools.reduce(jnp.add, [w * l for w, l in zip(ws, ls)])
        rows += [w * inv for w in ws]
    return jnp.concatenate(rows + [jnp.zeros((116, HEAD), F32)], axis=0).T


def merged(blocks, cols, h, at, size):
    total = None
    for j, b in enumerate(blocks):
        part = b[h * ROWS + at : h * ROWS + at + size, :].astype(F32)
        part = part * cols[:, 4 * h + j : 4 * h + j + 1]
        total = part if total is None else total + part
    return total


def merge_audio_body(p0, p1, p2, p3, out):
    blocks = (p0, p1, p2, p3)
    for t, size in enumerate((128, 128, 32)):
        cols = factors(blocks, t)
        for h in range(3):
            out[h, 128 * t : 128 * t + size, :] = merged(blocks, cols[:size], h, 128 * t, size)


def merge_body(p0, p1, p2, p3, extra, att_own, att_far):
    blocks = (p0, p1, p2, p3)
    audio = factors(blocks, 2)
    for r, att in ((1, att_far), (0, att_own)):
        video = factors(blocks, r)
        for h in range(3):
            for cols, at, size, to in (
                (video, 128 * r, 128, 0),
                (audio[16 * r : 16 * (r + 1)], 256 + 16 * r, 16, 128),
            ):
                total = extra[h, at : at + size, :] + merged(blocks, cols, h, at, size)
                att[h, to : to + size, :] = total.astype(BF)


def project_body(k, pos, att_own, att_near, wv, wa, out):
    c, y = pos[2], pos[3]
    rows = [pl.ds(pl.multiple_of(side * 384, 128), 384) for side in (c, 1 - c)]
    atts = [jnp.concatenate([a[h] for h in range(3)], axis=1) for a in (att_own, att_near)]
    cols = pl.ds(pl.multiple_of(((y + k) % 4) * 768, 128), 768)
    for lo, hi, w in ((0, 128, wv), (128, 144, wa)):
        part = jnp.dot(atts[0][lo:hi], w[rows[0], cols], preferred_element_type=F32)
        part += jnp.dot(atts[1][lo:hi], w[rows[1], cols], preferred_element_type=F32)
        out[lo:hi, :] = part.astype(BF)


def sum_body(p0, p1, p2, p3, video, audio):
    for out, lo, hi in ((video, 0, VBLK), (audio, VBLK, TOKENS)):
        ps = [p[lo:hi, :].astype(F32) for p in (p0, p1, p2, p3)]
        out[...] = ((ps[0] + ps[1]) + (ps[2] + ps[3])).astype(BF)


def moved(array, axis, by):
    n = lax.axis_size(axis)
    return lax.ppermute(array, axis, [(i, (i + by) % n) for i in range(n)])


def program(qv, kv, vv, qa, ka, va, video_spans, audio_spans, wv, wa):
    pos = jnp.stack([lax.axis_index(a) for a in ("x", "z", "c", "tp")]).astype(jnp.int32)
    spans = jnp.concatenate([audio_spans.reshape(-1), video_spans.reshape(-1)])
    block = pltpu.VMEM((VBLK, 768), BF)
    small = pltpu.VMEM((ABLK, 768), BF)
    own, far = kernel_call(
        entry_body, (((9, TOKENS, HEAD), BF),) * 2, [SSPEC] + [HSPEC] * 6, 2,
        scratch=[block, block, block, small, small, small, pltpu.SemaphoreType.DMA((6,))],
        vmem=66000000,
    )(pos, qv, kv, vv, qa, ka, va)
    near = moved(far, "c", 1)
    q_chip, kv_chip, audio = kernel_call(
        chip_body,
        (((3, ROWS, HEAD), BF), ((2, 6, TOKENS, HEAD), BF), ((6, 32, HEAD), BF)),
        [VSPEC] * 2, 0.5,
    )(own, near)
    audio_far = moved(audio, "z", 4)

    ups, downs = [kv_chip], [kv_chip]
    for _ in range(3):
        ups.append(moved(ups[-1], "z", 1))
        downs.append(moved(downs[-1], "z", -1))
    ups.append(moved(ups[3][:1], "z", 1))
    downs.append(moved(downs[3][1:], "z", -1))

    q_x = [q_chip] + [moved(q_chip, "x", k) for k in range(1, NX)]

    def both(dz, at):
        return [(dz, 0, at, 0), (dz, 1, at, 1)]

    groups = [
        ((kv_chip, ups[1], downs[1]), both(0, 0) + both(-1, 1) + both(1, 2)),
        ((ups[2], downs[2]), both(-2, 0) + both(2, 1)),
        ((ups[3], downs[3]), both(-3, 0) + both(3, 1)),
    ]
    state_shape = (((3, ROWS, HEAD), F32),) * 12
    state = ()
    for i, (arrays, blocks) in enumerate(groups):
        n = len(arrays)
        body = functools.partial(ring_body, blocks, (0, 1, 2, 3), i == 0, False)
        aliases = {} if i == 0 else {6 + n + j: j for j in range(12)}
        state = kernel_call(
            body, state_shape, [SSPEC] * 2 + [VSPEC] * (4 + n + len(state)), len(blocks), aliases
        )(pos, spans, *q_x, *arrays, *state)

    aparts = kernel_call(
        audio_body, (((PAYLOAD, HEAD), BF),) * 4, [SSPEC] * 2 + [VSPEC] * 12, 4,
        scratch=[pltpu.VMEM((NX, ROWS, HEAD), F32)],
    )(pos, spans, *q_x, kv_chip, ups[1], downs[1], ups[2], downs[2], ups[3], downs[3], audio_far)
    aback = [aparts[0]] + [moved(aparts[k], "x", -k) for k in range(1, NX)]

    final = [(-4, 0, 0, 0), (4, 1, 1, 0)]
    packed = kernel_call(
        functools.partial(ring_body, final, (0, 1, 2, 3), False, True),
        (((PAYLOAD, HEAD), BF),) * 4, [SSPEC] * 2 + [VSPEC] * 18, 4,
        scratch=[pltpu.VMEM((NX, ROWS, HEAD), F32)],
    )(pos, spans, *q_x, ups[4], downs[4], *state)
    back = [packed[0]] + [None] * 3
    for k in (2, 1, 3):
        back[k] = moved(packed[k], "x", -k)

    (extra,) = kernel_call(merge_audio_body, (((3, ROWS, HEAD), F32),), [VSPEC] * 4, 1)(*aback)
    att_own, att_far = kernel_call(
        merge_body, (((3, TOKENS, HEAD), BF),) * 2, [VSPEC] * 5, 1
    )(*back, extra)
    att_near = moved(att_far, "c", 1)
    parts = []
    for k in (2, 1, 3, 0):
        (part,) = kernel_call(
            functools.partial(project_body, k), (((TOKENS, 768), BF),), [SSPEC] + [VSPEC] * 4, 1,
        )(pos, att_own, att_near, wv, wa)
        parts.append(moved(part, "tp", k) if k else part)
    return kernel_call(sum_body, (((VBLK, 768), BF), ((ABLK, 768), BF)), [VSPEC] * 4, 0.5)(*parts)


def solution(mesh):
    finer = Mesh(mesh.devices.reshape(mesh.shape["tp"], NX, NZ, 2), ("tp", "x", "z", "c"))
    row = P(SEQ, "tp")
    in_specs = (row,) * 6 + (P(), P()) + (P("tp", None),) * 2
    return jax.shard_map(
        program, mesh=finer, in_specs=in_specs, out_specs=(row, row), check_vma=False
    )
```

```python
import functools
import math

import jax
import jax.numpy as jnp
from jax import lax
from jax.experimental import pallas as pl
from jax.experimental.pallas import tpu as pltpu
from jax.sharding import Mesh
from jax.sharding import PartitionSpec as P

HEAD = 128
VBLK = 128
ABLK = 16
ROWS = 2 * (VBLK + ABLK)
NX = 4
NZ = 8
SEQ = ("x", "z", "c")
SCALE = math.log2(math.e) / math.sqrt(HEAD)
MASKED = -1e30
LOWEST = -1e29
BF = jnp.bfloat16
F32 = jnp.float32
STATS = 3 * ROWS
PAYLOAD = STATS + 48
TOKENS = VBLK + ABLK


VSPEC = pl.BlockSpec(memory_space=pltpu.VMEM)
SSPEC = pl.BlockSpec(memory_space=pltpu.SMEM)
HSPEC = pl.BlockSpec(memory_space=pltpu.HBM)


def kernel_call(body, outs, in_specs, micros, aliases=None, scratch=(), vmem=32 << 20):
    shapes = tuple(jax.ShapeDtypeStruct(s, d) for s, d in outs)
    return pl.pallas_call(
        body,
        out_shape=shapes,
        in_specs=in_specs,
        out_specs=tuple(VSPEC for _ in shapes),
        scratch_shapes=scratch,
        input_output_aliases=aliases or {},
        cost_estimate=pl.CostEstimate(
            flops=int(micros * 1e9), bytes_accessed=1 << 16, transcendentals=0
        ),
        compiler_params=pltpu.CompilerParams(vmem_limit_bytes=vmem),
    )


def placed(body):
    def run(*refs):
        body(tuple(lax.axis_index(a) for a in ("x", "z", "c", "tp")), *refs)

    return run


def entry_body(
    pos, q_hbm, k_hbm, v_hbm, qa_hbm, ka_hbm, va_hbm, own, far, q, k, v, qa, ka, va, sems,
):
    pairs = ((k_hbm, k), (v_hbm, v), (q_hbm, q), (ka_hbm, ka), (va_hbm, va), (qa_hbm, qa))
    copies = [pltpu.make_async_copy(s, d, sems.at[i]) for i, (s, d) in enumerate(pairs)]
    for cp in copies:
        cp.start()
    for cp in copies:
        cp.wait()
    core = pos[2]
    for half, out in ((1, far), (0, own)):
        side = core if half == 0 else 1 - core
        for h in range(3):
            cols = pl.ds(pl.multiple_of((side * 3 + h) * HEAD, HEAD), HEAD)
            out[h, 0:VBLK, :] = k[:, cols].astype(F32).T.astype(BF)
            out[h, VBLK:TOKENS, :] = ka[:, cols]
            out[3 + h, 0:VBLK, :] = v[:, cols]
            out[3 + h, VBLK:TOKENS, :] = va[:, cols]
            out[6 + h, 0:VBLK, :] = q[:, cols]
            out[6 + h, VBLK:TOKENS, :] = qa[:, cols]


def chip_body(r, src, *refs):
    q_chip, kv_chip, audio = refs[-3:]
    kv_chip[r] = src[0:6]
    for i in range(6):
        audio[i, 16 * r : 16 * (r + 1), :] = src[i, VBLK:TOKENS, :]
    for h in range(3):
        q_chip[h, 128 * r : 128 * (r + 1), :] = src[6 + h, 0:VBLK, :]
        q_chip[h, 256 + 16 * r : 272 + 16 * r, :] = src[6 + h, VBLK:TOKENS, :]


def device_band(x, z, c):
    return (x * NZ + z) * 2 + c


def bf16_parts(a, count):
    parts = []
    for _ in range(count):
        parts.append(a.astype(BF).astype(F32))
        a = a - parts[-1]
    return parts


def ring_body(blocks, ks, first_call, last_call, *refs):
    n, nk = len(blocks), len(ks)
    pos, spans = refs[0], refs[1]
    qs = refs[2 : 2 + nk]
    n_kv = 1 + max(b[2] for b in blocks)
    kvs = [refs[2 + nk + at].at[place, :, 0:VBLK] for _, _, at, place in blocks]
    rest = refs[2 + nk + n_kv :]
    n_in = 0 if first_call else 3 * nk
    ins, outs = rest[:n_in], rest[n_in:]
    x, z, c = pos[0], pos[1], pos[2]
    key_bands = [
        device_band(x, (z + dz + NZ) % NZ, c if dc == 0 else 1 - c) for dz, dc, _, _ in blocks
    ]
    biases = {}
    for i, k in enumerate(ks):
        for r in range(2):
            band = device_band((x - k + NX) % NX, z, c if r == 0 else 1 - c)
            for j, b in enumerate(key_bands):
                ok = jnp.logical_and(spans[2 * band] <= b, b < spans[2 * band + 1])
                biases[i, r, j] = jnp.where(ok, 0.0, MASKED).astype(F32)

    def absorb(h):
        q = jnp.concatenate([qs[i][h] for i in range(nk)], axis=0)
        s = jnp.dot(q, jnp.concatenate([kv[h] for kv in kvs], axis=1), preferred_element_type=F32)
        tops, shifts, totals, ws = [], [], [], []
        for i in range(nk):
            at = i * ROWS
            parts = []
            for j in range(n):
                p = s[at : at + ROWS, 128 * j : 128 * (j + 1)]
                parts.append(
                    jnp.concatenate(
                        [p[:256], p[256:272] + biases[i, 0, j], p[272:288] + biases[i, 1, j]], axis=0
                    )
                )
            top = jnp.max(functools.reduce(jnp.maximum, parts), axis=1, keepdims=True)
            m_old = LOWEST if first_call else ins[3 * i][h]
            m_new = jnp.maximum(jnp.broadcast_to(top, (ROWS, HEAD)), m_old)
            shift = m_new * SCALE
            weights = [jnp.exp2(p * SCALE - shift) for p in parts]
            tops.append(m_new)
            shifts.append(shift)
            totals.append(functools.reduce(jnp.add, weights))
            ws.append(jnp.concatenate([w.astype(BF) for w in weights], axis=1))
        v = jnp.concatenate([kv[3 + h] for kv in kvs], axis=0)
        acc = jnp.dot(jnp.concatenate(ws, axis=0), v, preferred_element_type=F32)
        found = []
        for i in range(nk):
            part, total = acc[i * ROWS : (i + 1) * ROWS], totals[i]
            if not first_call:
                alpha = jnp.exp2(ins[3 * i][h] * SCALE - shifts[i])
                total = total + alpha * ins[3 * i + 1][h]
                part = part + alpha * ins[3 * i + 2][h]
            found.append((tops[i], total, part))
        return found

    if not last_call:

        def step(h, carry):
            for i, found in enumerate(absorb(h)):
                for j in range(3):
                    outs[3 * i + j][h] = found[j]
            return carry

        lax.fori_loop(0, 3, step, 0)
        return

    stats = outs[nk]
    lane = lax.broadcasted_iota(jnp.int32, (ROWS, HEAD), 1)

    def step(h, carry):
        for i, (m, l, acc) in enumerate(absorb(h)):
            outs[i][pl.ds(pl.multiple_of(h * ROWS, 16), ROWS), :] = acc.astype(BF)
            l = jnp.sum(l, axis=1, keepdims=True)
            stats[i] = jnp.where(lane == h, m, jnp.where(lane == 3 + h, l, stats[i]))
        return carry

    stats[...] = jnp.zeros_like(stats)
    lax.fori_loop(0, 3, step, 0)
    for i in range(nk):
        write_stats(outs[i], stats[i])


def write_stats(out, stats):
    tiles = [stats[0:128], stats[128:256]]
    tiles.append(jnp.concatenate([stats[256:288], jnp.zeros((96, HEAD), F32)], axis=0))
    for t, tile in enumerate(tiles):
        rows = tile.T
        parts = []
        for h in range(3):
            parts += bf16_parts(rows[h : h + 1], 3) + bf16_parts(rows[3 + h : 4 + h], 2)
        parts.append(jnp.zeros((1, HEAD), F32))
        out[STATS + 16 * t : STATS + 16 * (t + 1), :] = jnp.concatenate(parts, axis=0).astype(BF)


def audio_body(pos, spans, q0, q1, q2, q3, near, u1, d1, u2, d2, u3, d3, far, o0, o1, o2, o3, stats):
    x, z, c = pos[0], pos[1], pos[2]
    arrays = ((near, 0), (u1, -1), (d1, 1), (u2, -2), (d2, 2), (u3, -3), (d3, 3))
    group = lax.broadcasted_iota(jnp.int32, (1, 256), 1) // ABLK
    bands = jnp.zeros((1, 256), jnp.int32)
    places = [(dz, dc) for _, dz in arrays for dc in range(2)] + [(4, 0), (4, 1)]
    for g, (dz, dc) in enumerate(places):
        band = device_band(x, (z + dz + NZ) % NZ, c if dc == 0 else 1 - c)
        bands = jnp.where(group == g, band, bands)
    biases = []
    for k in range(NX):
        for r in range(2):
            mine = device_band((x - k + NX) % NX, z, c if r == 0 else 1 - c)
            ok = (bands >= spans[128 + 2 * mine]) & (bands < spans[129 + 2 * mine])
            biases.append(jnp.where(ok, 0.0, MASKED))
    lane = lax.broadcasted_iota(jnp.int32, (ROWS, HEAD), 1)
    stats[...] = jnp.zeros_like(stats)

    def head(h, carry):
        def rows_of(i):
            return jnp.concatenate(
                [a[r, i, VBLK:TOKENS, :] for a, _ in arrays for r in range(2)] + [far[i]], axis=0
            )

        keys, values = rows_of(h), rows_of(3 + h)
        q = jnp.concatenate([q0[h], q1[h], q2[h], q3[h]], axis=0)
        scores = lax.dot_general(q, keys, (((1,), (1,)), ((), ())), preferred_element_type=F32)
        ws = []
        for k in range(NX):
            s = scores[k * ROWS : (k + 1) * ROWS]
            s = jnp.concatenate(
                [s[0:128] + biases[2 * k], s[128:256] + biases[2 * k + 1], s[256:288]], axis=0
            )
            top = jnp.maximum(s[:, 0:128], s[:, 128:256])
            m = jnp.maximum(jnp.max(top, axis=1, keepdims=True), LOWEST)
            w = jnp.exp2(s * SCALE - m * SCALE)
            l = jnp.sum(w[:, 0:128] + w[:, 128:256], axis=1, keepdims=True)
            ws.append(w.astype(BF))
            stats[k] = jnp.where(lane == h, m, jnp.where(lane == 3 + h, l, stats[k]))
        acc = jnp.dot(jnp.concatenate(ws, axis=0), values, preferred_element_type=F32)
        for k, out in enumerate((o0, o1, o2, o3)):
            out[pl.ds(pl.multiple_of(h * ROWS, 16), ROWS), :] = acc[k * ROWS : (k + 1) * ROWS].astype(BF)
        return carry

    lax.fori_loop(0, 3, head, 0)
    for k, out in enumerate((o0, o1, o2, o3)):
        write_stats(out, stats[k])


def factors(blocks, t):
    stats = [b[STATS + 16 * t : STATS + 16 * (t + 1), :].astype(F32) for b in blocks]
    rows = []
    for h in range(3):
        at = 5 * h
        ms = [(s[at : at + 1] + s[at + 1 : at + 2]) + s[at + 2 : at + 3] for s in stats]
        ls = [s[at + 3 : at + 4] + s[at + 4 : at + 5] for s in stats]
        top = functools.reduce(jnp.maximum, ms)
        ws = [jnp.exp2((m - top) * SCALE) for m in ms]
        inv = 1.0 / functools.reduce(jnp.add, [w * l for w, l in zip(ws, ls)])
        rows += [w * inv for w in ws]
    return jnp.concatenate(rows + [jnp.zeros((116, HEAD), F32)], axis=0).T


def merged(blocks, cols, h, at, size):
    total = None
    for j, b in enumerate(blocks):
        part = b[h * ROWS + at : h * ROWS + at + size, :].astype(F32)
        part = part * cols[:, 4 * h + j : 4 * h + j + 1]
        total = part if total is None else total + part
    return total


def merge_audio_body(p0, p1, p2, p3, out):
    blocks = (p0, p1, p2, p3)
    for t, size in enumerate((128, 128, 32)):
        cols = factors(blocks, t)
        for h in range(3):
            out[h, 128 * t : 128 * t + size, :] = merged(blocks, cols[:size], h, 128 * t, size)


def merge_body(p0, p1, p2, p3, extra, att_own, att_far):
    blocks = (p0, p1, p2, p3)
    audio = factors(blocks, 2)
    for r, att in ((1, att_far), (0, att_own)):
        video = factors(blocks, r)
        for h in range(3):
            for cols, at, size, to in (
                (video, 128 * r, 128, 0),
                (audio[16 * r : 16 * (r + 1)], 256 + 16 * r, 16, 128),
            ):
                total = extra[h, at : at + size, :] + merged(blocks, cols, h, at, size)
                att[h, to : to + size, :] = total.astype(BF)


def project_body(k, pos, att_own, att_near, wv, wa, out):
    c, y = pos[2], pos[3]
    rows = [pl.ds(pl.multiple_of(side * 384, 128), 384) for side in (c, 1 - c)]
    atts = [jnp.concatenate([a[h] for h in range(3)], axis=1) for a in (att_own, att_near)]
    cols = pl.ds(pl.multiple_of(((y + k) % 4) * 768, 128), 768)
    for lo, hi, w in ((0, 128, wv), (128, 144, wa)):
        part = jnp.dot(atts[0][lo:hi], w[rows[0], cols], preferred_element_type=F32)
        part += jnp.dot(atts[1][lo:hi], w[rows[1], cols], preferred_element_type=F32)
        out[lo:hi, :] = part.astype(BF)


def sum_body(p0, p1, p2, p3, video, audio):
    for out, lo, hi in ((video, 0, VBLK), (audio, VBLK, TOKENS)):
        ps = [p[lo:hi, :].astype(F32) for p in (p0, p1, p2, p3)]
        out[...] = ((ps[0] + ps[1]) + (ps[2] + ps[3])).astype(BF)


def moved(array, axis, by):
    n = lax.axis_size(axis)
    return lax.ppermute(array, axis, [(i, (i + by) % n) for i in range(n)])


def program(qv, kv, vv, qa, ka, va, video_spans, audio_spans, wv, wa):
    spans = jnp.concatenate([audio_spans.reshape(-1), video_spans.reshape(-1)])
    block = pltpu.VMEM((VBLK, 768), BF)
    small = pltpu.VMEM((ABLK, 768), BF)
    own, far = kernel_call(
        placed(entry_body), (((9, TOKENS, HEAD), BF),) * 2, [HSPEC] * 6, 2,
        scratch=[block, block, block, small, small, small, pltpu.SemaphoreType.DMA((6,))],
        vmem=66000000,
    )(qv, kv, vv, qa, ka, va)
    near = moved(far, "c", 1)
    chip_shapes = (((3, ROWS, HEAD), BF), ((2, 6, TOKENS, HEAD), BF), ((6, 32, HEAD), BF))
    halves = kernel_call(functools.partial(chip_body, 0), chip_shapes, [VSPEC], 0.5)(own)
    q_chip, kv_chip, audio = kernel_call(
        functools.partial(chip_body, 1), chip_shapes, [VSPEC] * 4, 0.5, {1: 0, 2: 1, 3: 2}
    )(near, *halves)
    audio_far = moved(audio, "z", 4)

    ups, downs = [kv_chip], [kv_chip]
    for _ in range(3):
        ups.append(moved(ups[-1], "z", 1))
        downs.append(moved(downs[-1], "z", -1))
    ups.append(moved(ups[3][:1], "z", 1))
    downs.append(moved(downs[3][1:], "z", -1))

    q_x = [q_chip] + [moved(q_chip, "x", k) for k in range(1, NX)]

    def both(dz, at):
        return [(dz, 0, at, 0), (dz, 1, at, 1)]

    groups = [
        ((kv_chip, ups[1], downs[1]), both(0, 0) + both(-1, 1) + both(1, 2)),
        ((ups[2], downs[2]), both(-2, 0) + both(2, 1)),
    ]
    state_shape = (((3, ROWS, HEAD), F32),) * 12
    state = ()
    for i, (arrays, blocks) in enumerate(groups):
        n = len(arrays)
        body = placed(functools.partial(ring_body, blocks, (0, 1, 2, 3), i == 0, False))
        aliases = {} if i == 0 else {5 + n + j: j for j in range(12)}
        state = kernel_call(
            body, state_shape, [SSPEC] + [VSPEC] * (4 + n + len(state)), len(blocks), aliases
        )(spans, *q_x, *arrays, *state)

    aparts = kernel_call(
        placed(audio_body), (((PAYLOAD, HEAD), BF),) * 4, [SSPEC] + [VSPEC] * 12, 4,
        scratch=[pltpu.VMEM((NX, ROWS, HEAD), F32)],
    )(spans, *q_x, kv_chip, ups[1], downs[1], ups[2], downs[2], ups[3], downs[3], audio_far)
    aback = [aparts[0]] + [moved(aparts[k], "x", -k) for k in range(1, NX)]

    final = both(-3, 0) + both(3, 1) + [(-4, 0, 2, 0), (4, 1, 3, 0)]
    packed = kernel_call(
        placed(functools.partial(ring_body, final, (0, 1, 2, 3), False, True)),
        (((PAYLOAD, HEAD), BF),) * 4, [SSPEC] + [VSPEC] * 20, 6,
        scratch=[pltpu.VMEM((NX, ROWS, HEAD), F32)],
    )(spans, *q_x, ups[3], downs[3], ups[4], downs[4], *state)
    back = [packed[0]] + [None] * 3
    for k in (2, 1, 3):
        back[k] = moved(packed[k], "x", -k)

    (extra,) = kernel_call(merge_audio_body, (((3, ROWS, HEAD), F32),), [VSPEC] * 4, 1)(*aback)
    att_own, att_far = kernel_call(merge_body, (((3, TOKENS, HEAD), BF),) * 2, [VSPEC] * 5, 1)(*back, extra)
    att_near = moved(att_far, "c", 1)
    parts = []
    for k in (2, 1, 3, 0):
        (part,) = kernel_call(
            placed(functools.partial(project_body, k)), (((TOKENS, 768), BF),), [VSPEC] * 4, 1,
        )(att_own, att_near, wv, wa)
        parts.append(moved(part, "tp", k) if k else part)
    return kernel_call(sum_body, (((VBLK, 768), BF), ((ABLK, 768), BF)), [VSPEC] * 4, 0.5)(*parts)


def solution(mesh):
    finer = Mesh(mesh.devices.reshape(mesh.shape["tp"], NX, NZ, 2), ("tp", "x", "z", "c"))
    row = P(SEQ, "tp")
    in_specs = (row,) * 6 + (P(), P()) + (P("tp", None),) * 2
    return jax.shard_map(program, mesh=finer, in_specs=in_specs, out_specs=(row, row), check_vma=False)
```

```python
import functools
import math

import jax
import jax.numpy as jnp
from jax import lax
from jax.experimental import pallas as pl
from jax.experimental.pallas import tpu as pltpu
from jax.sharding import Mesh
from jax.sharding import PartitionSpec as P

HEAD = 128
VBLK = 128
ABLK = 16
ROWS = 2 * (VBLK + ABLK)
NX = 4
NZ = 8
SEQ = ("x", "z", "c")
SCALE = math.log2(math.e) / math.sqrt(HEAD)
MASKED = -1e30
LOWEST = -1e29
BF = jnp.bfloat16
F32 = jnp.float32
STATS = 3 * ROWS
PAYLOAD = STATS + 48
TOKENS = VBLK + ABLK


VSPEC = pl.BlockSpec(memory_space=pltpu.VMEM)
SSPEC = pl.BlockSpec(memory_space=pltpu.SMEM)
HSPEC = pl.BlockSpec(memory_space=pltpu.HBM)


def kernel_call(body, outs, in_specs, micros, aliases=None, scratch=(), vmem=32 << 20):
    shapes = tuple(jax.ShapeDtypeStruct(s, d) for s, d in outs)
    return pl.pallas_call(
        body,
        out_shape=shapes,
        in_specs=in_specs,
        out_specs=tuple(VSPEC for _ in shapes),
        scratch_shapes=scratch,
        input_output_aliases=aliases or {},
        cost_estimate=pl.CostEstimate(
            flops=int(micros * 1e9), bytes_accessed=1 << 16, transcendentals=0
        ),
        compiler_params=pltpu.CompilerParams(vmem_limit_bytes=vmem),
    )


def placed(body):
    def run(*refs):
        body(tuple(lax.axis_index(a) for a in ("x", "z", "c", "tp")), *refs)

    return run


def entry_body(
    pos, q_hbm, k_hbm, v_hbm, qa_hbm, ka_hbm, va_hbm, own, far, q, k, v, qa, ka, va, sems,
):
    pairs = ((k_hbm, k), (v_hbm, v), (q_hbm, q), (ka_hbm, ka), (va_hbm, va), (qa_hbm, qa))
    copies = [pltpu.make_async_copy(s, d, sems.at[i]) for i, (s, d) in enumerate(pairs)]
    for cp in copies:
        cp.start()
    for cp in copies:
        cp.wait()
    core = pos[2]
    for half, out in ((1, far), (0, own)):
        side = core if half == 0 else 1 - core
        for h in range(3):
            cols = pl.ds(pl.multiple_of((side * 3 + h) * HEAD, HEAD), HEAD)
            out[h, 0:VBLK, :] = k[:, cols].astype(F32).T.astype(BF)
            out[h, VBLK:TOKENS, :] = ka[:, cols]
            out[3 + h, 0:VBLK, :] = v[:, cols]
            out[3 + h, VBLK:TOKENS, :] = va[:, cols]
            out[6 + h, 0:VBLK, :] = q[:, cols]
            out[6 + h, VBLK:TOKENS, :] = qa[:, cols]


def chip_body(r, src, *refs):
    q_chip, kv_chip, audio = refs[-3:]
    kv_chip[r] = src[0:6]
    for i in range(6):
        audio[i, 16 * r : 16 * (r + 1), :] = src[i, VBLK:TOKENS, :]
    for h in range(3):
        q_chip[h, 128 * r : 128 * (r + 1), :] = src[6 + h, 0:VBLK, :]
        q_chip[h, 256 + 16 * r : 272 + 16 * r, :] = src[6 + h, VBLK:TOKENS, :]


def device_band(x, z, c):
    return (x * NZ + z) * 2 + c


def bf16_parts(a, count):
    parts = []
    for _ in range(count):
        parts.append(a.astype(BF).astype(F32))
        a = a - parts[-1]
    return parts


def ring_body(blocks, ks, first_call, last_call, *refs):
    n, nk = len(blocks), len(ks)
    pos, spans = refs[0], refs[1]
    qs = refs[2 : 2 + nk]
    n_kv = 1 + max(b[2] for b in blocks)
    kvs = [refs[2 + nk + at].at[place, :, 0:VBLK] for _, _, at, place in blocks]
    rest = refs[2 + nk + n_kv :]
    n_in = 0 if first_call else 3 * nk
    ins, outs = rest[:n_in], rest[n_in:]
    x, z, c = pos[0], pos[1], pos[2]
    key_bands = [
        device_band(x, (z + dz + NZ) % NZ, c if dc == 0 else 1 - c) for dz, dc, _, _ in blocks
    ]
    biases = {}
    for i, k in enumerate(ks):
        for r in range(2):
            band = device_band((x - k + NX) % NX, z, c if r == 0 else 1 - c)
            for j, b in enumerate(key_bands):
                ok = jnp.logical_and(spans[2 * band] <= b, b < spans[2 * band + 1])
                biases[i, r, j] = jnp.where(ok, 0.0, MASKED).astype(F32)

    def absorb(h):
        q = jnp.concatenate([qs[i][h] for i in range(nk)], axis=0)
        s = jnp.dot(q, jnp.concatenate([kv[h] for kv in kvs], axis=1), preferred_element_type=F32)
        tops, shifts, totals, ws = [], [], [], []
        for i in range(nk):
            at = i * ROWS
            parts = []
            for j in range(n):
                p = s[at : at + ROWS, 128 * j : 128 * (j + 1)]
                parts.append(
                    jnp.concatenate(
                        [p[:256], p[256:272] + biases[i, 0, j], p[272:288] + biases[i, 1, j]], axis=0
                    )
                )
            top = jnp.max(functools.reduce(jnp.maximum, parts), axis=1, keepdims=True)
            m_old = LOWEST if first_call else ins[3 * i][h]
            m_new = jnp.maximum(jnp.broadcast_to(top, (ROWS, HEAD)), m_old)
            shift = m_new * SCALE
            weights = [jnp.exp2(p * SCALE - shift) for p in parts]
            tops.append(m_new)
            shifts.append(shift)
            totals.append(functools.reduce(jnp.add, weights))
            ws.append(jnp.concatenate([w.astype(BF) for w in weights], axis=1))
        v = jnp.concatenate([kv[3 + h] for kv in kvs], axis=0)
        acc = jnp.dot(jnp.concatenate(ws, axis=0), v, preferred_element_type=F32)
        found = []
        for i in range(nk):
            part, total = acc[i * ROWS : (i + 1) * ROWS], totals[i]
            if not first_call:
                alpha = jnp.exp2(ins[3 * i][h] * SCALE - shifts[i])
                total = total + alpha * ins[3 * i + 1][h]
                part = part + alpha * ins[3 * i + 2][h]
            found.append((tops[i], total, part))
        return found

    if not last_call:

        def step(h, carry):
            for i, found in enumerate(absorb(h)):
                for j in range(3):
                    outs[3 * i + j][h] = found[j]
            return carry

        for h in range(3):
            step(h, 0)
        return

    stats = outs[nk]
    lane = lax.broadcasted_iota(jnp.int32, (ROWS, HEAD), 1)

    def step(h, carry):
        for i, (m, l, acc) in enumerate(absorb(h)):
            outs[i][pl.ds(pl.multiple_of(h * ROWS, 16), ROWS), :] = acc.astype(BF)
            l = jnp.sum(l, axis=1, keepdims=True)
            stats[i] = jnp.where(lane == h, m, jnp.where(lane == 3 + h, l, stats[i]))
        return carry

    stats[...] = jnp.zeros_like(stats)
    for h in range(3):
        step(h, 0)
    for i in range(nk):
        write_stats(outs[i], stats[i])


def write_stats(out, stats):
    tiles = [stats[0:128], stats[128:256]]
    tiles.append(jnp.concatenate([stats[256:288], jnp.zeros((96, HEAD), F32)], axis=0))
    for t, tile in enumerate(tiles):
        rows = tile.T
        parts = []
        for h in range(3):
            parts += bf16_parts(rows[h : h + 1], 3) + bf16_parts(rows[3 + h : 4 + h], 2)
        parts.append(jnp.zeros((1, HEAD), F32))
        out[STATS + 16 * t : STATS + 16 * (t + 1), :] = jnp.concatenate(parts, axis=0).astype(BF)


def audio_body(pos, spans, q0, q1, q2, q3, near, u1, d1, u2, d2, u3, d3, far, o0, o1, o2, o3, stats):
    x, z, c = pos[0], pos[1], pos[2]
    arrays = ((near, 0), (u1, -1), (d1, 1), (u2, -2), (d2, 2), (u3, -3), (d3, 3))
    group = lax.broadcasted_iota(jnp.int32, (1, 256), 1) // ABLK
    bands = jnp.zeros((1, 256), jnp.int32)
    places = [(dz, dc) for _, dz in arrays for dc in range(2)] + [(4, 0), (4, 1)]
    for g, (dz, dc) in enumerate(places):
        band = device_band(x, (z + dz + NZ) % NZ, c if dc == 0 else 1 - c)
        bands = jnp.where(group == g, band, bands)
    biases = []
    for k in range(NX):
        for r in range(2):
            mine = device_band((x - k + NX) % NX, z, c if r == 0 else 1 - c)
            ok = (bands >= spans[128 + 2 * mine]) & (bands < spans[129 + 2 * mine])
            biases.append(jnp.where(ok, 0.0, MASKED))
    lane = lax.broadcasted_iota(jnp.int32, (ROWS, HEAD), 1)
    stats[...] = jnp.zeros_like(stats)

    def head(h, carry):
        def rows_of(i):
            return jnp.concatenate(
                [a[r, i, VBLK:TOKENS, :] for a, _ in arrays for r in range(2)] + [far[i]], axis=0
            )

        keys, values = rows_of(h), rows_of(3 + h)
        q = jnp.concatenate([q0[h], q1[h], q2[h], q3[h]], axis=0)
        scores = lax.dot_general(q, keys, (((1,), (1,)), ((), ())), preferred_element_type=F32)
        ws = []
        for k in range(NX):
            s = scores[k * ROWS : (k + 1) * ROWS]
            s = jnp.concatenate(
                [s[0:128] + biases[2 * k], s[128:256] + biases[2 * k + 1], s[256:288]], axis=0
            )
            top = jnp.maximum(s[:, 0:128], s[:, 128:256])
            m = jnp.maximum(jnp.max(top, axis=1, keepdims=True), LOWEST)
            w = jnp.exp2(s * SCALE - m * SCALE)
            l = jnp.sum(w[:, 0:128] + w[:, 128:256], axis=1, keepdims=True)
            ws.append(w.astype(BF))
            stats[k] = jnp.where(lane == h, m, jnp.where(lane == 3 + h, l, stats[k]))
        acc = jnp.dot(jnp.concatenate(ws, axis=0), values, preferred_element_type=F32)
        for k, out in enumerate((o0, o1, o2, o3)):
            out[pl.ds(pl.multiple_of(h * ROWS, 16), ROWS), :] = acc[k * ROWS : (k + 1) * ROWS].astype(BF)
        return carry

    for h in range(3):
        head(h, 0)
    for k, out in enumerate((o0, o1, o2, o3)):
        write_stats(out, stats[k])


def factors(blocks, t):
    stats = [b[STATS + 16 * t : STATS + 16 * (t + 1), :].astype(F32) for b in blocks]
    rows = []
    for h in range(3):
        at = 5 * h
        ms = [(s[at : at + 1] + s[at + 1 : at + 2]) + s[at + 2 : at + 3] for s in stats]
        ls = [s[at + 3 : at + 4] + s[at + 4 : at + 5] for s in stats]
        top = functools.reduce(jnp.maximum, ms)
        ws = [jnp.exp2((m - top) * SCALE) for m in ms]
        inv = 1.0 / functools.reduce(jnp.add, [w * l for w, l in zip(ws, ls)])
        rows += [w * inv for w in ws]
    return jnp.concatenate(rows + [jnp.zeros((116, HEAD), F32)], axis=0).T


def merged(blocks, cols, h, at, size):
    total = None
    for j, b in enumerate(blocks):
        part = b[h * ROWS + at : h * ROWS + at + size, :].astype(F32)
        part = part * cols[:, 4 * h + j : 4 * h + j + 1]
        total = part if total is None else total + part
    return total


def merge_audio_body(p0, p1, p2, p3, out):
    blocks = (p0, p1, p2, p3)
    for t, size in enumerate((128, 128, 32)):
        cols = factors(blocks, t)
        for h in range(3):
            out[h, 128 * t : 128 * t + size, :] = merged(blocks, cols[:size], h, 128 * t, size)


def merge_body(p0, p1, p2, p3, extra, att_own, att_far):
    blocks = (p0, p1, p2, p3)
    audio = factors(blocks, 2)
    for r, att in ((1, att_far), (0, att_own)):
        video = factors(blocks, r)
        for h in range(3):
            for cols, at, size, to in (
                (video, 128 * r, 128, 0),
                (audio[16 * r : 16 * (r + 1)], 256 + 16 * r, 16, 128),
            ):
                total = extra[h, at : at + size, :] + merged(blocks, cols, h, at, size)
                att[h, to : to + size, :] = total.astype(BF)


def project_body(k, pos, att_own, att_near, wv, wa, out):
    c, y = pos[2], pos[3]
    rows = [pl.ds(pl.multiple_of(side * 384, 128), 384) for side in (c, 1 - c)]
    atts = [jnp.concatenate([a[h] for h in range(3)], axis=1) for a in (att_own, att_near)]
    cols = pl.ds(pl.multiple_of(((y + k) % 4) * 768, 128), 768)
    for lo, hi, w in ((0, 128, wv), (128, 144, wa)):
        part = jnp.dot(atts[0][lo:hi], w[rows[0], cols], preferred_element_type=F32)
        part += jnp.dot(atts[1][lo:hi], w[rows[1], cols], preferred_element_type=F32)
        out[lo:hi, :] = part.astype(BF)


def sum_body(p0, p1, p2, p3, video, audio):
    for out, lo, hi in ((video, 0, VBLK), (audio, VBLK, TOKENS)):
        ps = [p[lo:hi, :].astype(F32) for p in (p0, p1, p2, p3)]
        out[...] = ((ps[0] + ps[1]) + (ps[2] + ps[3])).astype(BF)


def moved(array, axis, by):
    n = lax.axis_size(axis)
    return lax.ppermute(array, axis, [(i, (i + by) % n) for i in range(n)])


def program(qv, kv, vv, qa, ka, va, video_spans, audio_spans, wv, wa):
    spans = jnp.concatenate([audio_spans.reshape(-1), video_spans.reshape(-1)])
    block = pltpu.VMEM((VBLK, 768), BF)
    small = pltpu.VMEM((ABLK, 768), BF)
    own, far = kernel_call(
        placed(entry_body), (((9, TOKENS, HEAD), BF),) * 2, [HSPEC] * 6, 2,
        scratch=[block, block, block, small, small, small, pltpu.SemaphoreType.DMA((6,))],
        vmem=66000000,
    )(qv, kv, vv, qa, ka, va)
    near = moved(far, "c", 1)
    chip_shapes = (((3, ROWS, HEAD), BF), ((2, 6, TOKENS, HEAD), BF), ((6, 32, HEAD), BF))
    halves = kernel_call(functools.partial(chip_body, 0), chip_shapes, [VSPEC], 0.5)(own)
    q_chip, kv_chip, audio = kernel_call(
        functools.partial(chip_body, 1), chip_shapes, [VSPEC] * 4, 0.5, {1: 0, 2: 1, 3: 2}
    )(near, *halves)
    audio_far = moved(audio, "z", 4)

    ups, downs = [kv_chip], [kv_chip]
    for _ in range(3):
        ups.append(moved(ups[-1], "z", 1))
        downs.append(moved(downs[-1], "z", -1))
    ups.append(moved(ups[3][:1], "z", 1))
    downs.append(moved(downs[3][1:], "z", -1))

    q_x = [q_chip] + [moved(q_chip, "x", k) for k in range(1, NX)]

    def both(dz, at):
        return [(dz, 0, at, 0), (dz, 1, at, 1)]

    groups = [
        ((kv_chip, ups[1], downs[1]), both(0, 0) + both(-1, 1) + both(1, 2)),
        ((ups[2], downs[2]), both(-2, 0) + both(2, 1)),
    ]
    state_shape = (((3, ROWS, HEAD), F32),) * 12
    state = ()
    for i, (arrays, blocks) in enumerate(groups):
        n = len(arrays)
        body = placed(functools.partial(ring_body, blocks, (0, 1, 2, 3), i == 0, False))
        aliases = {} if i == 0 else {5 + n + j: j for j in range(12)}
        state = kernel_call(
            body, state_shape, [SSPEC] + [VSPEC] * (4 + n + len(state)), len(blocks), aliases
        )(spans, *q_x, *arrays, *state)

    aparts = kernel_call(
        placed(audio_body), (((PAYLOAD, HEAD), BF),) * 4, [SSPEC] + [VSPEC] * 12, 4,
        scratch=[pltpu.VMEM((NX, ROWS, HEAD), F32)],
    )(spans, *q_x, kv_chip, ups[1], downs[1], ups[2], downs[2], ups[3], downs[3], audio_far)
    aback = [aparts[0]] + [moved(aparts[k], "x", -k) for k in range(1, NX)]

    final = both(-3, 0) + both(3, 1) + [(-4, 0, 2, 0), (4, 1, 3, 0)]
    packed = kernel_call(
        placed(functools.partial(ring_body, final, (0, 1, 2, 3), False, True)),
        (((PAYLOAD, HEAD), BF),) * 4, [SSPEC] + [VSPEC] * 20, 6,
        scratch=[pltpu.VMEM((NX, ROWS, HEAD), F32)],
    )(spans, *q_x, ups[3], downs[3], ups[4], downs[4], *state)
    back = [packed[0]] + [None] * 3
    for k in (2, 1, 3):
        back[k] = moved(packed[k], "x", -k)

    (extra,) = kernel_call(merge_audio_body, (((3, ROWS, HEAD), F32),), [VSPEC] * 4, 1)(*aback)
    att_own, att_far = kernel_call(merge_body, (((3, TOKENS, HEAD), BF),) * 2, [VSPEC] * 5, 1)(*back, extra)
    att_near = moved(att_far, "c", 1)
    parts = []
    for k in (2, 1, 3, 0):
        (part,) = kernel_call(
            placed(functools.partial(project_body, k)), (((TOKENS, 768), BF),), [VSPEC] * 4, 1,
        )(att_own, att_near, wv, wa)
        parts.append(moved(part, "tp", k) if k else part)
    return kernel_call(sum_body, (((VBLK, 768), BF), ((ABLK, 768), BF)), [VSPEC] * 4, 0.5)(*parts)


def solution(mesh):
    finer = Mesh(mesh.devices.reshape(mesh.shape["tp"], NX, NZ, 2), ("tp", "x", "z", "c"))
    row = P(SEQ, "tp")
    in_specs = (row,) * 6 + (P(), P()) + (P("tp", None),) * 2
    return jax.shard_map(program, mesh=finer, in_specs=in_specs, out_specs=(row, row), check_vma=False)
```

```python
import functools
import math

import jax
import jax.numpy as jnp
from jax import lax
from jax.experimental import pallas as pl
from jax.experimental.pallas import tpu as pltpu
from jax.sharding import Mesh
from jax.sharding import PartitionSpec as P

HEAD = 128
VBLK = 128
ABLK = 16
ROWS = 2 * (VBLK + ABLK)
NX = 4
NZ = 8
SEQ = ("x", "z", "c")
SCALE = math.log2(math.e) / math.sqrt(HEAD)
MASKED = -1e30
LOWEST = -1e29
BF = jnp.bfloat16
F32 = jnp.float32
STATS = 3 * ROWS
PAYLOAD = STATS + 48
TOKENS = VBLK + ABLK


VSPEC = pl.BlockSpec(memory_space=pltpu.VMEM)
SSPEC = pl.BlockSpec(memory_space=pltpu.SMEM)
HSPEC = pl.BlockSpec(memory_space=pltpu.HBM)


def kernel_call(body, outs, in_specs, micros, aliases=None, scratch=(), vmem=32 << 20):
    shapes = tuple(jax.ShapeDtypeStruct(s, d) for s, d in outs)
    return pl.pallas_call(
        body,
        out_shape=shapes,
        in_specs=in_specs,
        out_specs=tuple(VSPEC for _ in shapes),
        scratch_shapes=scratch,
        input_output_aliases=aliases or {},
        cost_estimate=pl.CostEstimate(
            flops=int(micros * 1e9), bytes_accessed=1 << 16, transcendentals=0
        ),
        compiler_params=pltpu.CompilerParams(vmem_limit_bytes=vmem),
    )


def placed(body):
    def run(*refs):
        body(tuple(lax.axis_index(a) for a in ("x", "z", "c", "tp")), *refs)

    return run


def entry_body(
    pos, q_hbm, k_hbm, v_hbm, qa_hbm, ka_hbm, va_hbm, own, far, q, k, v, qa, ka, va, sems,
):
    pairs = ((k_hbm, k), (v_hbm, v), (q_hbm, q), (ka_hbm, ka), (va_hbm, va), (qa_hbm, qa))
    copies = [pltpu.make_async_copy(s, d, sems.at[i]) for i, (s, d) in enumerate(pairs)]
    for cp in copies:
        cp.start()
    core = pos[2]

    def targets():
        for half, out in ((1, far), (0, own)):
            side = core if half == 0 else 1 - core
            for h in range(3):
                yield out, h, pl.ds(pl.multiple_of((side * 3 + h) * HEAD, HEAD), HEAD)

    copies[0].wait()
    for out, h, cols in targets():
        out[h, 0:VBLK, :] = k[:, cols].astype(F32).T.astype(BF)
    for cp in copies[1:]:
        cp.wait()
    for out, h, cols in targets():
        out[h, VBLK:TOKENS, :] = ka[:, cols]
        out[3 + h, 0:VBLK, :] = v[:, cols]
        out[3 + h, VBLK:TOKENS, :] = va[:, cols]
        out[6 + h, 0:VBLK, :] = q[:, cols]
        out[6 + h, VBLK:TOKENS, :] = qa[:, cols]


def chip_body(r, src, *refs):
    q_chip, kv_chip, audio = refs[-3:]
    kv_chip[r] = src[0:6]
    for i in range(6):
        audio[i, 16 * r : 16 * (r + 1), :] = src[i, VBLK:TOKENS, :]
    for h in range(3):
        q_chip[h, 128 * r : 128 * (r + 1), :] = src[6 + h, 0:VBLK, :]
        q_chip[h, 256 + 16 * r : 272 + 16 * r, :] = src[6 + h, VBLK:TOKENS, :]


def device_band(x, z, c):
    return (x * NZ + z) * 2 + c


def bf16_parts(a, count):
    parts = []
    for _ in range(count):
        parts.append(a.astype(BF).astype(F32))
        a = a - parts[-1]
    return parts


def ring_body(blocks, ks, first_call, last_call, *refs):
    n, nk = len(blocks), len(ks)
    pos, spans = refs[0], refs[1]
    qs = refs[2 : 2 + nk]
    n_kv = 1 + max(b[2] for b in blocks)
    kvs = [refs[2 + nk + at].at[place, :, 0:VBLK] for _, _, at, place in blocks]
    rest = refs[2 + nk + n_kv :]
    n_in = 0 if first_call else 3 * nk
    ins, outs = rest[:n_in], rest[n_in:]
    x, z, c = pos[0], pos[1], pos[2]
    key_bands = [
        device_band(x, (z + dz + NZ) % NZ, c if dc == 0 else 1 - c) for dz, dc, _, _ in blocks
    ]
    biases = {}
    for i, k in enumerate(ks):
        for r in range(2):
            band = device_band((x - k + NX) % NX, z, c if r == 0 else 1 - c)
            for j, b in enumerate(key_bands):
                ok = jnp.logical_and(spans[2 * band] <= b, b < spans[2 * band + 1])
                biases[i, r, j] = jnp.where(ok, 0.0, MASKED).astype(F32)

    def absorb(h):
        q = jnp.concatenate([qs[i][h] for i in range(nk)], axis=0)
        s = jnp.dot(q, jnp.concatenate([kv[h] for kv in kvs], axis=1), preferred_element_type=F32)
        tops, shifts, totals, ws = [], [], [], []
        for i in range(nk):
            at = i * ROWS
            parts = []
            for j in range(n):
                p = s[at : at + ROWS, 128 * j : 128 * (j + 1)]
                parts.append(
                    jnp.concatenate(
                        [p[:256], p[256:272] + biases[i, 0, j], p[272:288] + biases[i, 1, j]], axis=0
                    )
                )
            top = jnp.max(functools.reduce(jnp.maximum, parts), axis=1, keepdims=True)
            m_old = LOWEST if first_call else ins[3 * i][h]
            m_new = jnp.maximum(jnp.broadcast_to(top, (ROWS, HEAD)), m_old)
            shift = m_new * SCALE
            weights = [jnp.exp2(p * SCALE - shift) for p in parts]
            tops.append(m_new)
            shifts.append(shift)
            totals.append(functools.reduce(jnp.add, weights))
            ws.append(jnp.concatenate([w.astype(BF) for w in weights], axis=1))
        v = jnp.concatenate([kv[3 + h] for kv in kvs], axis=0)
        acc = jnp.dot(jnp.concatenate(ws, axis=0), v, preferred_element_type=F32)
        found = []
        for i in range(nk):
            part, total = acc[i * ROWS : (i + 1) * ROWS], totals[i]
            if not first_call:
                alpha = jnp.exp2(ins[3 * i][h] * SCALE - shifts[i])
                total = total + alpha * ins[3 * i + 1][h]
                part = part + alpha * ins[3 * i + 2][h]
            found.append((tops[i], total, part))
        return found

    if not last_call:

        def step(h, carry):
            for i, found in enumerate(absorb(h)):
                for j in range(3):
                    outs[3 * i + j][h] = found[j]
            return carry

        for h in range(3):
            step(h, 0)
        return

    stats = outs[nk]
    lane = lax.broadcasted_iota(jnp.int32, (ROWS, HEAD), 1)

    def step(h, carry):
        for i, (m, l, acc) in enumerate(absorb(h)):
            outs[i][pl.ds(pl.multiple_of(h * ROWS, 16), ROWS), :] = acc.astype(BF)
            l = jnp.sum(l, axis=1, keepdims=True)
            stats[i] = jnp.where(lane == h, m, jnp.where(lane == 3 + h, l, stats[i]))
        return carry

    stats[...] = jnp.zeros_like(stats)
    for h in range(3):
        step(h, 0)
    for i in range(nk):
        write_stats(outs[i], stats[i])


def write_stats(out, stats):
    tiles = [stats[0:128], stats[128:256]]
    tiles.append(jnp.concatenate([stats[256:288], jnp.zeros((96, HEAD), F32)], axis=0))
    for t, tile in enumerate(tiles):
        rows = tile.T
        parts = []
        for h in range(3):
            parts += bf16_parts(rows[h : h + 1], 3) + bf16_parts(rows[3 + h : 4 + h], 2)
        parts.append(jnp.zeros((1, HEAD), F32))
        out[STATS + 16 * t : STATS + 16 * (t + 1), :] = jnp.concatenate(parts, axis=0).astype(BF)


def audio_body(pos, spans, q0, q1, q2, q3, near, u1, d1, u2, d2, u3, d3, far, o0, o1, o2, o3, stats):
    x, z, c = pos[0], pos[1], pos[2]
    arrays = ((near, 0), (u1, -1), (d1, 1), (u2, -2), (d2, 2), (u3, -3), (d3, 3))
    group = lax.broadcasted_iota(jnp.int32, (1, 256), 1) // ABLK
    bands = jnp.zeros((1, 256), jnp.int32)
    places = [(dz, dc) for _, dz in arrays for dc in range(2)] + [(4, 0), (4, 1)]
    for g, (dz, dc) in enumerate(places):
        band = device_band(x, (z + dz + NZ) % NZ, c if dc == 0 else 1 - c)
        bands = jnp.where(group == g, band, bands)
    biases = []
    for k in range(NX):
        for r in range(2):
            mine = device_band((x - k + NX) % NX, z, c if r == 0 else 1 - c)
            ok = (bands >= spans[128 + 2 * mine]) & (bands < spans[129 + 2 * mine])
            biases.append(jnp.where(ok, 0.0, MASKED))
    lane = lax.broadcasted_iota(jnp.int32, (ROWS, HEAD), 1)
    stats[...] = jnp.zeros_like(stats)

    def head(h, carry):
        def rows_of(i):
            return jnp.concatenate(
                [a[r, i, VBLK:TOKENS, :] for a, _ in arrays for r in range(2)] + [far[i]], axis=0
            )

        keys, values = rows_of(h), rows_of(3 + h)
        q = jnp.concatenate([q0[h], q1[h], q2[h], q3[h]], axis=0)
        scores = lax.dot_general(q, keys, (((1,), (1,)), ((), ())), preferred_element_type=F32)
        ws = []
        for k in range(NX):
            s = scores[k * ROWS : (k + 1) * ROWS]
            s = jnp.concatenate(
                [s[0:128] + biases[2 * k], s[128:256] + biases[2 * k + 1], s[256:288]], axis=0
            )
            top = jnp.maximum(s[:, 0:128], s[:, 128:256])
            m = jnp.maximum(jnp.max(top, axis=1, keepdims=True), LOWEST)
            w = jnp.exp2(s * SCALE - m * SCALE)
            l = jnp.sum(w[:, 0:128] + w[:, 128:256], axis=1, keepdims=True)
            ws.append(w.astype(BF))
            stats[k] = jnp.where(lane == h, m, jnp.where(lane == 3 + h, l, stats[k]))
        acc = jnp.dot(jnp.concatenate(ws, axis=0), values, preferred_element_type=F32)
        for k, out in enumerate((o0, o1, o2, o3)):
            out[pl.ds(pl.multiple_of(h * ROWS, 16), ROWS), :] = acc[k * ROWS : (k + 1) * ROWS].astype(BF)
        return carry

    for h in range(3):
        head(h, 0)
    for k, out in enumerate((o0, o1, o2, o3)):
        write_stats(out, stats[k])


def factors(blocks, t):
    stats = [b[STATS + 16 * t : STATS + 16 * (t + 1), :].astype(F32) for b in blocks]
    rows = []
    for h in range(3):
        at = 5 * h
        ms = [(s[at : at + 1] + s[at + 1 : at + 2]) + s[at + 2 : at + 3] for s in stats]
        ls = [s[at + 3 : at + 4] + s[at + 4 : at + 5] for s in stats]
        top = functools.reduce(jnp.maximum, ms)
        ws = [jnp.exp2((m - top) * SCALE) for m in ms]
        inv = 1.0 / functools.reduce(jnp.add, [w * l for w, l in zip(ws, ls)])
        rows += [w * inv for w in ws]
    return jnp.concatenate(rows + [jnp.zeros((116, HEAD), F32)], axis=0).T


def merged(blocks, cols, h, at, size):
    total = None
    for j, b in enumerate(blocks):
        part = b[h * ROWS + at : h * ROWS + at + size, :].astype(F32)
        part = part * cols[:, 4 * h + j : 4 * h + j + 1]
        total = part if total is None else total + part
    return total


def merge_audio_body(p0, p1, p2, p3, out):
    blocks = (p0, p1, p2, p3)
    for t, size in enumerate((128, 128, 32)):
        cols = factors(blocks, t)
        for h in range(3):
            out[h, 128 * t : 128 * t + size, :] = merged(blocks, cols[:size], h, 128 * t, size)


def merge_body(p0, p1, p2, p3, extra, att_own, att_far):
    blocks = (p0, p1, p2, p3)
    audio = factors(blocks, 2)
    for r, att in ((1, att_far), (0, att_own)):
        video = factors(blocks, r)
        for h in range(3):
            for cols, at, size, to in (
                (video, 128 * r, 128, 0),
                (audio[16 * r : 16 * (r + 1)], 256 + 16 * r, 16, 128),
            ):
                total = extra[h, at : at + size, :] + merged(blocks, cols, h, at, size)
                att[h, to : to + size, :] = total.astype(BF)


def project_body(k, pos, att_own, att_near, wv, wa, out):
    c, y = pos[2], pos[3]
    rows = [pl.ds(pl.multiple_of(side * 384, 128), 384) for side in (c, 1 - c)]
    atts = [jnp.concatenate([a[h] for h in range(3)], axis=1) for a in (att_own, att_near)]
    cols = pl.ds(pl.multiple_of(((y + k) % 4) * 768, 128), 768)
    for lo, hi, w in ((0, 128, wv), (128, 144, wa)):
        part = jnp.dot(atts[0][lo:hi], w[rows[0], cols], preferred_element_type=F32)
        part += jnp.dot(atts[1][lo:hi], w[rows[1], cols], preferred_element_type=F32)
        out[lo:hi, :] = part.astype(BF)


def sum_body(p0, p1, p2, p3, video, audio):
    for out, lo, hi in ((video, 0, VBLK), (audio, VBLK, TOKENS)):
        ps = [p[lo:hi, :].astype(F32) for p in (p0, p1, p2, p3)]
        out[...] = ((ps[0] + ps[1]) + (ps[2] + ps[3])).astype(BF)


def moved(array, axis, by):
    n = lax.axis_size(axis)
    return lax.ppermute(array, axis, [(i, (i + by) % n) for i in range(n)])


def program(qv, kv, vv, qa, ka, va, video_spans, audio_spans, wv, wa):
    spans = jnp.concatenate([audio_spans.reshape(-1), video_spans.reshape(-1)])
    block = pltpu.VMEM((VBLK, 768), BF)
    small = pltpu.VMEM((ABLK, 768), BF)
    own, far = kernel_call(
        placed(entry_body), (((9, TOKENS, HEAD), BF),) * 2, [HSPEC] * 6, 2,
        scratch=[block, block, block, small, small, small, pltpu.SemaphoreType.DMA((6,))],
        vmem=66000000,
    )(qv, kv, vv, qa, ka, va)
    near = moved(far, "c", 1)
    chip_shapes = (((3, ROWS, HEAD), BF), ((2, 6, TOKENS, HEAD), BF), ((6, 32, HEAD), BF))
    halves = kernel_call(functools.partial(chip_body, 0), chip_shapes, [VSPEC], 0.5)(own)
    q_chip, kv_chip, audio = kernel_call(
        functools.partial(chip_body, 1), chip_shapes, [VSPEC] * 4, 0.5, {1: 0, 2: 1, 3: 2}
    )(near, *halves)
    audio_far = moved(audio, "z", 4)

    ups, downs = [kv_chip], [kv_chip]
    for _ in range(3):
        ups.append(moved(ups[-1], "z", 1))
        downs.append(moved(downs[-1], "z", -1))
    ups.append(moved(ups[3][:1], "z", 1))
    downs.append(moved(downs[3][1:], "z", -1))

    q_x = [q_chip] + [moved(q_chip, "x", k) for k in range(1, NX)]

    def both(dz, at):
        return [(dz, 0, at, 0), (dz, 1, at, 1)]

    groups = [
        ((kv_chip, ups[1], downs[1]), both(0, 0) + both(-1, 1) + both(1, 2)),
        ((ups[2], downs[2]), both(-2, 0) + both(2, 1)),
    ]
    state_shape = (((3, ROWS, HEAD), F32),) * 12
    state = ()
    for i, (arrays, blocks) in enumerate(groups):
        n = len(arrays)
        body = placed(functools.partial(ring_body, blocks, (0, 1, 2, 3), i == 0, False))
        aliases = {} if i == 0 else {5 + n + j: j for j in range(12)}
        state = kernel_call(
            body, state_shape, [SSPEC] + [VSPEC] * (4 + n + len(state)), len(blocks), aliases
        )(spans, *q_x, *arrays, *state)

    aparts = kernel_call(
        placed(audio_body), (((PAYLOAD, HEAD), BF),) * 4, [SSPEC] + [VSPEC] * 12, 4,
        scratch=[pltpu.VMEM((NX, ROWS, HEAD), F32)],
    )(spans, *q_x, kv_chip, ups[1], downs[1], ups[2], downs[2], ups[3], downs[3], audio_far)
    aback = [aparts[0]] + [moved(aparts[k], "x", -k) for k in range(1, NX)]

    final = both(-3, 0) + both(3, 1) + [(-4, 0, 2, 0), (4, 1, 3, 0)]
    packed = kernel_call(
        placed(functools.partial(ring_body, final, (0, 1, 2, 3), False, True)),
        (((PAYLOAD, HEAD), BF),) * 4, [SSPEC] + [VSPEC] * 20, 6,
        scratch=[pltpu.VMEM((NX, ROWS, HEAD), F32)],
    )(spans, *q_x, ups[3], downs[3], ups[4], downs[4], *state)
    back = [packed[0]] + [None] * 3
    for k in (2, 1, 3):
        back[k] = moved(packed[k], "x", -k)

    (extra,) = kernel_call(merge_audio_body, (((3, ROWS, HEAD), F32),), [VSPEC] * 4, 1)(*aback)
    att_own, att_far = kernel_call(merge_body, (((3, TOKENS, HEAD), BF),) * 2, [VSPEC] * 5, 1)(*back, extra)
    att_near = moved(att_far, "c", 1)
    parts = []
    for k in (2, 1, 3, 0):
        (part,) = kernel_call(
            placed(functools.partial(project_body, k)), (((TOKENS, 768), BF),), [VSPEC] * 4, 1,
        )(att_own, att_near, wv, wa)
        parts.append(moved(part, "tp", k) if k else part)
    return kernel_call(sum_body, (((VBLK, 768), BF), ((ABLK, 768), BF)), [VSPEC] * 4, 0.5)(*parts)


def solution(mesh):
    finer = Mesh(mesh.devices.reshape(mesh.shape["tp"], NX, NZ, 2), ("tp", "x", "z", "c"))
    row = P(SEQ, "tp")
    in_specs = (row,) * 6 + (P(), P()) + (P("tp", None),) * 2
    return jax.shard_map(program, mesh=finer, in_specs=in_specs, out_specs=(row, row), check_vma=False)
```
